128 devices in a mesh: slab: 8 (over x, y_hi), plane: 16 (over z, y_lo, core).
Axes of the slice: x: 4, y: 4 (y_hi: 2, y_lo: 2; y = y_hi * 2 + y_lo), z: 4, core: 2. Of those that a mesh axis runs over, the one named last changes fastest.
Arguments:
- images: float32 [2, 64, 256, 1024], P(None, 'slab', 'plane'), may hold values from -12 to 12, as said below
- shifts: int32 [3, 8, 32, 128], P(None, 'slab', 'plane'), may hold values from -1 to 1
- initial_displacement: float32 [3, 8, 32, 128], P(None, 'slab', 'plane'), may hold values from -2 to 2
Outputs:
- displacement: float32 [3, 8, 32, 128], P(None, 'slab', 'plane')
- mismatch: float32 [64, 256, 1024], P('slab', 'plane')
The draws below stay inside these ranges and needn't reach their ends.
Inputs may be any that keep to these rules, and one draw needn't show every extreme that they name: `images`: voxel intensities.
All inputs are finite; a program needn't handle non-finite values.
Results may differ from the reference program's by a relative error of at most 0.0023.
Values sent between devices are 32-bit elements; how exact they have to be, the bound alone decides.
No kernel may reach another device: no remote copies, remote signals or barrier semaphores. Data moves between devices by JAX's collectives and lax.ppermute only.
A program may use at most 192 MiB of HBM per device.

```python
import jax
import jax.numpy as jnp

ELEM = 8
ITERS = 6
NX = 1024
NZ = 64
NY = 256
ELEMENT_LAYERS = 8
ELEMENT_ROWS = 32
ELEMENTS_ACROSS = 128


def draw_images(key, part):
    depth_frac = (jnp.arange(NZ, dtype=jnp.float32) + 0.5) / NZ
    height_frac = (jnp.arange(NY, dtype=jnp.float32) + 0.5) / NY
    noise = jnp.clip(jax.random.normal(key, (2, NZ, NY, NX), jnp.float32), -4.0, 4.0)
    scales = 3.0 ** (depth_frac[:, None] + height_frac[None, :]) / 3.0
    return scales[None, :, :, None] * noise


def place_ends(values, key, low, top_value):
    shape = values.shape
    index_at = [jax.random.randint(jax.random.fold_in(key, axis), (), 0, shape[axis]) for axis in range(len(shape))]
    values = values.at[tuple(index_at)].set(low)
    longest = shape.index(max(shape))
    index_at[longest] = (index_at[longest] + 1) % shape[longest]
    return values.at[tuple(index_at)].set(top_value)


def block_scale(rng, shape, cuts, low, largest):
    level = 1.0
    for position, blocks in cuts:
        draws = jax.random.uniform(jax.random.fold_in(jax.random.fold_in(rng, 6), position), (blocks,), jnp.float32, low / len(cuts), largest / len(cuts))
        level = level * jnp.repeat(jnp.exp(draws), shape[position] // blocks).reshape((-1,) + (1,) * (len(shape) - 1 - position))
    return level


def gaussian(own_key, dims, deviation, bound, pieces=(), kind=jnp.bfloat16):
    values = jax.random.normal(own_key, dims, jnp.float32) * deviation
    if len(pieces) > 0:
        values = block_scale(own_key, dims, pieces, -0.22, 0.18) * values
    return jnp.clip(values, min=-bound, max=bound).astype(kind)


def setup_inputs(seed: int = 0) -> dict:
    splits = jax.random.split(jax.random.key(seed), 4)
    return {
        "images": draw_images(jax.random.fold_in(splits[3], 71), 0),
        "shifts": place_ends(jax.random.randint(splits[1], (3, ELEMENT_LAYERS, ELEMENT_ROWS, ELEMENTS_ACROSS), -1, 2), jax.random.fold_in(splits[1], 1), -1, 1).astype(jnp.int32),
        "initial_displacement": gaussian(splits[2], (3, ELEMENT_LAYERS, ELEMENT_ROWS, ELEMENTS_ACROSS), 0.3, 2.0, ((1, 8), (2, 16)), jnp.float32),
    }


reg_weight = 4.0


def edge_weights():
    return jnp.arange(ELEM, dtype=jnp.float32) / ELEM


def interpolate(padded):
    weights = edge_weights()
    lower_w = 1.0 - weights
    comps, nodes_z, nodes_y, nodes_x = padded.shape
    depth_direction = padded[:, :-1, None] * lower_w[:, None, None] + padded[:, 1:, None] * weights[:, None, None]
    depth_direction = depth_direction.reshape(comps, (nodes_z - 1) * ELEM, nodes_y, nodes_x)
    along_y = depth_direction[:, :, :-1, None] * lower_w[:, None] + depth_direction[:, :, 1:, None] * weights[:, None]
    along_y = along_y.reshape(comps, (nodes_z - 1) * ELEM, (nodes_y - 1) * ELEM, nodes_x)
    along_x = along_y[..., :-1, None] * lower_w + along_y[..., 1:, None] * weights
    return along_x.reshape(comps, (nodes_z - 1) * ELEM, (nodes_y - 1) * ELEM, (nodes_x - 1) * ELEM)


def laplacian(padded):
    centre = padded[:, 1:-1, 1:-1, 1:-1]
    beside = padded[:, :-2, 1:-1, 1:-1] + padded[:, 2:, 1:-1, 1:-1]
    beside = beside + padded[:, 1:-1, :-2, 1:-1] + padded[:, 1:-1, 2:, 1:-1]
    beside = beside + padded[:, 1:-1, 1:-1, :-2] + padded[:, 1:-1, 1:-1, 2:]
    return 6.0 * centre - beside


def collapse_width(field):
    weights = edge_weights()
    comps, zcount, ycount, xcount = field.shape
    blocks = field.reshape(comps, zcount, ycount, xcount // ELEM, ELEM)
    lower = jnp.sum(blocks * (1.0 - weights), -1)
    upper = jnp.sum(blocks * weights, -1)
    return lower + jnp.concatenate([jnp.zeros_like(upper[..., :1]), upper[..., :-1]], -1)


def reduce_y(field):
    weights = edge_weights()
    comps, zcount, ycount, xcount = field.shape
    blocks = field.reshape(comps, zcount, ycount // ELEM, ELEM, xcount)
    lower = jnp.sum(blocks * (1.0 - weights)[:, None], 3)
    upper = jnp.sum(blocks * weights[:, None], 3)
    return lower, upper


def reduce_z(field):
    weights = edge_weights()
    comps, zcount, ycount, xcount = field.shape
    blocks = field.reshape(comps, zcount // ELEM, ELEM, ycount, xcount)
    lower = jnp.sum(blocks * (1.0 - weights)[:, None, None], 2)
    upper = jnp.sum(blocks * weights[:, None, None], 2)
    return lower, upper


def restrict(field):
    nodes_x = collapse_width(field)
    lower, upper = reduce_y(nodes_x)
    nodes_y = lower + jnp.concatenate([jnp.zeros_like(upper[:, :, :1]), upper[:, :, :-1]], 2)
    lower, upper = reduce_z(nodes_y)
    return lower + jnp.concatenate([jnp.zeros_like(upper[:, :1]), upper[:, :-1]], 1)


def gradient(padded, margin, zcount, ycount, xcount):
    def piece(off_z, off_y, off_x):
        return padded[margin + off_z:margin + off_z + zcount, margin + off_y:margin + off_y + ycount, margin + off_x:margin + off_x + xcount]

    grad_z = (piece(-2, 0, 0) - 8.0 * piece(-1, 0, 0) + 8.0 * piece(1, 0, 0) - piece(2, 0, 0)) / 12.0
    gradient_height = (piece(0, -2, 0) - 8.0 * piece(0, -1, 0) + 8.0 * piece(0, 1, 0) - piece(0, 2, 0)) / 12.0
    grad_x = (piece(0, 0, -2) - 8.0 * piece(0, 0, -1) + 8.0 * piece(0, 0, 1) - piece(0, 0, 2)) / 12.0
    return jnp.stack([grad_z, gradient_height, grad_x])


def voxel_codes(shifts):
    codes = (shifts[0] + 1) * 9 + (shifts[1] + 1) * 3 + (shifts[2] + 1)
    elem_z, elem_y, elem_x = codes.shape
    spread = jnp.broadcast_to(codes[:, None, :, None, :, None], (elem_z, ELEM, elem_y, ELEM, elem_x, ELEM))
    return spread.reshape(elem_z * ELEM, elem_y * ELEM, elem_x * ELEM).astype(jnp.int32)


def warp_image(padded, margin, codes):
    zcount, ycount, xcount = codes.shape
    result = jnp.zeros(codes.shape, padded.dtype)
    for candidate in range(27):
        off_z = candidate // 9 - 1
        off_y = (candidate // 3) % 3 - 1
        off_x = candidate % 3 - 1
        piece = padded[margin + off_z:margin + off_z + zcount, margin + off_y:margin + off_y + ycount, margin + off_x:margin + off_x + xcount]
        result = jnp.where(codes == candidate, piece, result)
    return result


def reference(images, shifts, initial_displacement):
    ref_img = images[0]
    codes = voxel_codes(shifts)
    grads = gradient(jnp.pad(ref_img, 2), 2, NZ, NY, NX)
    warped = warp_image(jnp.pad(images[1], 1), 1, codes)
    node_pad = jnp.pad(initial_displacement, ((0, 0), (1, 1), (1, 1), (1, 1)))
    moved = interpolate(node_pad[:, 1:, 1:, 1:])
    mismatch = ref_img - warped - jnp.sum(grads * moved, 0)
    energy = jnp.sum(grads * grads)
    smoothing_penalty = reg_weight * energy / (NZ * NY * NX)

    def apply_op(vector):
        vector_pad = jnp.pad(vector, ((0, 0), (1, 1), (1, 1), (1, 1)))
        flow = interpolate(vector_pad[:, 1:, 1:, 1:])
        scalar = jnp.sum(grads * flow, 0)
        return restrict(grads * scalar[None]) + smoothing_penalty * laplacian(vector_pad)

    rhs = restrict(grads * mismatch[None]) - smoothing_penalty * laplacian(node_pad)
    step = jnp.zeros_like(rhs)
    residual = rhs
    direction = rhs
    norm_now = jnp.sum(residual * residual)
    for sweep in range(ITERS):
        applied = apply_op(direction)
        step_size = norm_now / jnp.sum(direction * applied)
        step = step + step_size * direction
        residual = residual - step_size * applied
        norm_next = jnp.sum(residual * residual)
        direction = residual + (norm_next / norm_now) * direction
        norm_now = norm_next
    return initial_displacement + step, mismatch
```

```python
import jax
import jax.numpy as jnp
import numpy as np
from jax import lax
from jax.experimental import pallas as pl
from jax.experimental.pallas import tpu as pltpu
from jax.sharding import PartitionSpec as P

ELEM = 8
ITERS = 6
reg_weight = 4.0
AXES = ("slab", "plane")
NCHUNK = 8
ROWS = 112
RHS_ROW = 96
U_ROW = 102
ENERGY_ROW = 108
COLORS = ((0, 40), (40, 40), (80, 32))
STRIDE = 136
PAIRS = ((0, 0), (0, 1), (0, 2), (1, 1), (1, 2), (2, 2))
AB = [[0, 1, 2], [1, 3, 4], [2, 4, 5]]
F32 = jnp.float32
BF16 = jnp.bfloat16


def build_constants():
    w = np.arange(8) / 8.0
    lo, up = 1.0 - w, w
    quad = (lo * lo, lo * up, up * up)
    lin = (lo, up)
    wq = np.zeros((1024, 256))
    wl = np.zeros((1024, 128))
    for e in range(128):
        for i in range(8):
            v = 8 * e + i
            wq[v, e] += quad[0][i]
            wq[v, 128 + e] += quad[1][i]
            wl[v, e] += lin[0][i]
            if e + 1 < 128:
                wq[v, e + 1] += quad[2][i]
                wl[v, e + 1] += lin[1][i]
    spread = np.zeros((128, 1024))
    for e in range(128):
        spread[e, 8 * e : 8 * e + 8] = 1.0
    ly = np.zeros((4, 48, 288))
    ry = np.zeros((4, 8, 96))

    def put(which, tz, yk, zt, er, yq):
        for ab in range(6):
            for s in range(8):
                ly[which, (tz * 4 + yk) * 6 + ab, ((zt * 6 + ab) * 2 + er) * 8 + s] += quad[yq][s]

    for which, tz, zt in ((0, 0, 0), (0, 1, 1), (1, 0, 2)):
        put(which, tz, 0, zt, 0, 0)
        put(which, tz, 1, zt, 0, 2)
        put(which, tz, 1, zt, 1, 0)
        put(which, tz, 2, zt, 0, 1)
        put(which, tz, 3, zt, 1, 1)
    for which, tz, zt in ((2, 0, 0), (2, 1, 1), (3, 0, 2)):
        put(which, tz, 0, zt, 1, 2)

    def put_rhs(which, yl, zt, er, yq):
        for c in range(3):
            for s in range(8):
                ry[which, yl * 3 + c, ((zt * 3 + c) * 2 + er) * 8 + s] += lin[yq][s]

    for which, zt in ((0, 0), (1, 1)):
        put_rhs(which, 0, zt, 0, 0)
        put_rhs(which, 1, zt, 0, 1)
        put_rhs(which, 1, zt, 1, 0)
    for which, zt in ((2, 0), (3, 1)):
        put_rhs(which, 0, zt, 1, 1)
    cast = lambda a: jnp.asarray(a.astype(np.float32)).astype(BF16)
    return (
        cast(wq),
        cast(wl),
        cast(wl.T),
        cast(spread),
        cast(ly.reshape(192, 288)),
        cast(ry.reshape(32, 96)),
    )


def dot(a, b):
    return lax.dot_general(a, b, (((1,), (0,)), ((), ())), preferred_element_type=F32)


def split_left(a, b, parts=2):
    total = None
    for _ in range(parts):
        piece = a.astype(BF16)
        a = a - piece.astype(F32)
        term = dot(piece, b)
        total = term if total is None else total + term
    return total


def split_right(a, b, parts=2):
    total = None
    for _ in range(parts):
        piece = b.astype(BF16)
        b = b - piece.astype(F32)
        term = dot(a, piece)
        total = term if total is None else total + term
    return total


def local_kernel(
    images, zlo, zhi, ylo, yhi, shifts, nodes, wq, wl, wi, spread, ly, ry,
    mismatch, own, to_slab, to_plane, to_both,
    pad0, pad1, gx, sh, un, acc, acc_rhs,
):
    lane = lax.broadcasted_iota(jnp.int32, (1, 1024), 1)
    pad0[2:10, 8:24, :] = images[0]
    pad0[0:2, 8:24, :] = zlo[0:32, :].reshape(2, 16, 1024)
    pad0[10:12, 8:24, :] = zhi[0:32, :].reshape(2, 16, 1024)
    pad1[1, 0, 8:24, :] = zlo[32:48, :]
    pad1[1, 1:9, 8:24, :] = images[1]
    pad1[1, 9, 8:24, :] = zhi[32:48, :]
    for z in range(8):
        pad0[2 + z, 6:8, :] = ylo[2 * z : 2 * z + 2, :]
        pad0[2 + z, 24:26, :] = yhi[2 * z : 2 * z + 2, :]
    for k in range(10):
        pad1[1, k, 7:8, :] = ylo[16 + k : 17 + k, :]
        pad1[1, k, 24:25, :] = yhi[16 + k : 17 + k, :]

    def lanes(value, off):
        moved = pltpu.roll(value, (-off) % 1024, value.ndim - 1)
        inside = (lane + off >= 0) & (lane + off < 1024)
        return jnp.where(inside, moved, 0.0)

    def shift_planes(k, carry):
        plane = pad1[1, k]
        pad1[0, k] = lanes(plane, -1)
        pad1[2, k] = lanes(plane, 1)
        return carry

    lax.fori_loop(0, 10, shift_planes, 0)

    def along_x(z, carry):
        t = images[0, z]
        gx[z] = (lanes(t, -2) - lanes(t, 2) + 8.0 * (lanes(t, 1) - lanes(t, -1))) * (1.0 / 12.0)
        return carry

    lax.fori_loop(0, 8, along_x, 0)
    sh[...] = dot(shifts[...].astype(F32).astype(BF16), spread[...])
    un[...] = split_left(nodes[...], wi[...], 3)
    wy = lax.broadcasted_iota(jnp.int32, (8, 128), 0).astype(F32) * 0.125

    def chunk(c, energy):
        at = pl.ds(pl.multiple_of(c * 128, 128), 128)
        for er in range(2):
            base = 8 + 8 * er

            def full(row):
                return jnp.broadcast_to(row, (8, 128))

            sz = full(sh[er : er + 1, at])
            sy = full(sh[2 + er : 3 + er, at])
            sx = full(sh[4 + er : 5 + er, at])
            x_low, x_up = sx < -0.5, sx > 0.5
            y_low, y_up = sy < -0.5, sy > 0.5
            z_low, z_up = sz < -0.5, sz > 0.5

            def in_plane(k):
                rows = []
                for dy in (-1, 0, 1):
                    a, b, d = (pad1[i, k, base + dy : base + dy + 8, at] for i in range(3))
                    rows.append(jnp.where(x_low, a, jnp.where(x_up, d, b)))
                return jnp.where(y_low, rows[0], jnp.where(y_up, rows[2], rows[1]))

            corner = []
            for comp in range(3):
                for zn in range(2):
                    i = (comp * 2 + zn) * 3 + er
                    first, second = full(un[i : i + 1, at]), full(un[i + 1 : i + 2, at])
                    corner.append(first + wy * (second - first))
            sums = [None] * 18
            sums_rhs = [None] * 6
            planes = [in_plane(0), in_plane(1)]
            for z in range(8):
                planes.append(in_plane(z + 2))
                warped = jnp.where(z_low, planes[z], jnp.where(z_up, planes[z + 2], planes[z + 1]))
                here = lambda k: pad0[k, base : base + 8, at]
                rows = lambda dy: pad0[z + 2, base + dy : base + dy + 8, at]
                g0 = (here(z) - here(z + 4) + 8.0 * (here(z + 3) - here(z + 1))) * (1.0 / 12.0)
                g1 = (rows(-2) - rows(2) + 8.0 * (rows(1) - rows(-1))) * (1.0 / 12.0)
                g2 = gx[z, base - 8 : base, at]
                g = (g0, g1, g2)
                w = z / 8.0
                total = None
                for comp in range(3):
                    moved = corner[2 * comp] + w * (corner[2 * comp + 1] - corner[2 * comp])
                    term = g[comp] * moved
                    total = term if total is None else total + term
                mis = here(z + 2) - warped - total
                mismatch[z, base - 8 : base, at] = mis

                def add(store, i, weight, value):
                    if weight:
                        term = value if weight == 1.0 else weight * value
                        store[i] = term if store[i] is None else store[i] + term

                for ab, (a, b) in enumerate(PAIRS):
                    prod = g[a] * g[b]
                    if a == b:
                        energy = energy + prod
                    for zt, weight in enumerate(((1 - w) * (1 - w), w * (1 - w), w * w)):
                        add(sums, zt * 6 + ab, weight, prod)
                for comp in range(3):
                    prod = g[comp] * mis
                    for zt, weight in enumerate((1 - w, w)):
                        add(sums_rhs, zt * 3 + comp, weight, prod)
            for i in range(18):
                r = (i * 2 + er) * 8
                acc[r : r + 8, at] = sums[i]
            for i in range(6):
                r = (i * 2 + er) * 8
                acc_rhs[r : r + 8, at] = sums_rhs[i]
        return energy

    energy = lax.fori_loop(0, NCHUNK, chunk, jnp.zeros((8, 128), F32))
    by_x = split_left(acc[...], wq[...])
    by_x_rhs = split_left(acc_rhs[...], wl[...])
    by_y = split_right(ly[...], by_x)
    by_y_rhs = split_right(ry[...], by_x_rhs)
    for i, out in enumerate((own, to_slab, to_plane, to_both)):
        out[0:48, :] = by_y[48 * i : 48 * i + 48, 0:128]
        out[48:96, :] = by_y[48 * i : 48 * i + 48, 128:256]
        out[96:112, :] = jnp.zeros((16, 128), F32)
        out[96:102, :] = by_y_rhs[8 * i : 8 * i + 6, :]
    for yl in range(2):
        for comp in range(3):
            r = U_ROW + yl * 3 + comp
            i = comp * 6 + yl
            own[r : r + 1, :] = nodes[i : i + 1, :]
    own[ENERGY_ROW : ENERGY_ROW + 1, :] = jnp.sum(energy, axis=0, keepdims=True)


def local_part(images, zlo, zhi, ylo, yhi, shifts, nodes):
    vmem = pl.BlockSpec(memory_space=pltpu.VMEM)
    message = jax.ShapeDtypeStruct((ROWS, 128), F32)
    constants = build_constants()
    return pl.pallas_call(
        local_kernel,
        out_shape=(jax.ShapeDtypeStruct((8, 16, 1024), F32),) + (message,) * 4,
        in_specs=[vmem] * 13,
        out_specs=(vmem,) * 5,
        scratch_shapes=[
            pltpu.VMEM((12, 32, 1024), F32),
            pltpu.VMEM((3, 10, 32, 1024), F32),
            pltpu.VMEM((8, 16, 1024), F32),
            pltpu.VMEM((8, 1024), F32),
            pltpu.VMEM((24, 1024), F32),
            pltpu.VMEM((288, 1024), F32),
            pltpu.VMEM((96, 1024), F32),
        ],
        compiler_params=pltpu.CompilerParams(vmem_limit_bytes=40 << 20),
        name="local_part",
    )(images, zlo, zhi, ylo, yhi, shifts, nodes, *constants)


def solve_kernel(*refs):
    place, nodes = refs[0], refs[1]
    pieces = refs[2:14]
    out = refs[14]
    data, var, high, vec_x, vec_r, vec_p, vec_y = refs[15:]
    slab, plane = place[0], place[1]
    x_me, y_me = slab // 2, (slab % 2) * 2 + (plane // 2) % 2
    z_me, core = plane // 4, plane % 2

    def arrange(j, carry):
        for source in range(2):
            k = core if source == 0 else 1 - core
            first, second = 1 + 2 * k, 3 - 2 * k
            bits = [(j >> i) & 1 for i in range(5)]
            for color in range(3):
                start, count = COLORS[color]
                order = [(color + i) % 3 for i in range(3)]
                for half in range(2):
                    delta = [bits[0] * first, bits[1] * first, bits[2] * first]
                    delta[order[0]] = delta[order[0]] ^ (bits[3] * second)
                    delta[order[1]] = delta[order[1]] ^ (bits[4] * second)
                    if half:
                        delta[order[2]] = delta[order[2]] ^ second
                    x, y, z = x_me ^ delta[0], y_me ^ delta[1], z_me ^ delta[2]
                    device = (x * 2 + (y >> 1)) * 16 + z * 4 + (y & 1) * 2 + k
                    piece = pieces[(source * 2 + half) * 3 + color]
                    for t in range(count // 8):
                        r = (start + 8 * t) * STRIDE
                        data[pl.ds(r + device, 8, stride=STRIDE), :] = piece[j, 8 * t : 8 * t + 8, :]
        return carry

    lax.fori_loop(0, 32, arrange, 0)

    def field(r):
        return data[r * STRIDE : r * STRIDE + 128, :]

    total = jnp.sum(jnp.sum(field(ENERGY_ROW), axis=0, keepdims=True), axis=1, keepdims=True)
    penalty = reg_weight / (64.0 * 256.0 * 1024.0) * total

    def row_of(tx, tz, yk, ab):
        return ((tx * 2 + tz) * 4 + yk) * 6 + ab

    for ab in (0, 3, 5):
        for yk in range(2):
            for tx, tz, y_kind, weight in (
                (0, 0, yk, 6.0), (0, 0, 2 + yk, -1.0), (0, 1, yk, -1.0), (1, 0, yk, -1.0)
            ):
                r = row_of(tx, tz, y_kind, ab) * STRIDE
                data[r : r + 128, :] = data[r : r + 128, :] + weight * penalty

    lane = lax.broadcasted_iota(jnp.int32, (128, 128), 1)
    row = lax.broadcasted_iota(jnp.int32, (128, 128), 0)
    in_plane = row % 16

    def x_next(v):
        return jnp.where(lane < 127, pltpu.roll(v, 127, 1), 0.0)

    def x_prev(v):
        return jnp.where(lane > 0, pltpu.roll(v, 1, 1), 0.0)

    def p_next(v):
        return jnp.where(in_plane < 15, pltpu.roll(v, 127, 0), 0.0)

    def p_prev(v):
        return jnp.where(in_plane > 0, pltpu.roll(v, 1, 0), 0.0)

    zero = jnp.zeros((16, 128), F32)

    def z_next(v):
        return jnp.concatenate([v[16:], zero], axis=0)

    def z_prev(v):
        return jnp.concatenate([zero, v[:112]], axis=0)

    for comp in range(3):
        u = [field(U_ROW + yl * 3 + comp) for yl in range(2)]
        for yl in range(2):
            v = u[yl]
            beside = z_next(v) + z_prev(v) + x_next(v) + x_prev(v)
            beside = beside + (u[1] + p_prev(u[1]) if yl == 0 else u[0] + p_next(u[0]))
            rhs = field(RHS_ROW + yl * 3 + comp) - penalty * (6.0 * v - beside)
            i = comp * 2 + yl
            vec_r[i] = rhs
            vec_p[i] = rhs
            vec_x[i] = jnp.zeros((128, 128), F32)

    def norm():
        value = None
        for i in range(6):
            term = vec_r[i] * vec_r[i]
            value = term if value is None else value + term
        return jnp.sum(jnp.sum(value, axis=0, keepdims=True), axis=1, keepdims=True)

    var[8] = jnp.zeros((18, 16, 128), F32)
    lane16 = lax.broadcasted_iota(jnp.int32, (16, 128), 1)
    row16 = lax.broadcasted_iota(jnp.int32, (16, 128), 0)

    def multiply(z, energy):
        here = pl.ds(pl.multiple_of(z * 16, 16), 16)
        values = [
            [var[z + dz, i] for i in range(18)] for dz in range(2)
        ]

        def mat(tx, tz, yk, ab):
            start = row_of(tx, tz, yk, ab) * STRIDE
            return data[pl.ds(pl.multiple_of(start + z * 16, 8), 16), :]

        def accumulate(z_out, y_out, x_out):
            sums = [high[3 * (y_out * 2 + x_out) + a] if z_out == 0 else None for a in range(3)]
            for tz in range(2):
                if tz == 0 and z_out == 1:
                    continue
                z_in = 0 if tz == 0 else 1 - z_out
                for tx in range(2):
                    if tx == 0 and x_out == 1:
                        continue
                    x_in = 0 if tx == 0 else 1 - x_out
                    if y_out == 0:
                        kinds = ((0, 0), (2, 1))
                    elif y_out == 1:
                        kinds = ((1, 1), (2, 0), (3, 2))
                    else:
                        kinds = ((3, 1),)
                    for yk, y_in in kinds:
                        m = [mat(tx, tz, yk, ab) for ab in range(6)]
                        v = [values[z_in][(b * 3 + y_in) * 2 + x_in] for b in range(3)]
                        for a in range(3):
                            term = m[AB[a][0]] * v[0] + m[AB[a][1]] * v[1] + m[AB[a][2]] * v[2]
                            sums[a] = term if sums[a] is None else sums[a] + term
            return sums

        lows = [[accumulate(0, y_out, x_out) for x_out in range(2)] for y_out in range(3)]
        for a in range(3):
            parts = [
                lows[y][0][a] + jnp.where(lane16 > 0, pltpu.roll(lows[y][1][a], 1, 1), 0.0)
                for y in range(3)
            ]
            down = jnp.where(row16 > 0, pltpu.roll(parts[2], 1, 0), 0.0)
            result = (parts[0] + down, parts[1])
            for yl in range(2):
                vec_y[a * 2 + yl, here, :] = result[yl]
                energy = energy + result[yl] * values[0][(a * 3 + yl) * 2]
        for y_out in range(3):
            for x_out in range(2):
                sums = accumulate(1, y_out, x_out)
                for a in range(3):
                    high[3 * (y_out * 2 + x_out) + a] = sums[a]
        return energy

    def sweep(step, norm_now):
        for comp in range(3):
            own = [vec_p[comp * 2 + yl] for yl in range(2)]
            for y_kind, v in enumerate((own[0], own[1], p_next(own[0]))):
                i = (comp * 3 + y_kind) * 2
                var[0:8, i] = v.reshape(8, 16, 128)
                var[0:8, i + 1] = x_next(v).reshape(8, 16, 128)
        high[...] = jnp.zeros((18, 16, 128), F32)
        energy = lax.fori_loop(0, 8, multiply, jnp.zeros((16, 128), F32))
        curvature = jnp.sum(jnp.sum(energy, axis=0, keepdims=True), axis=1, keepdims=True)
        size = norm_now / curvature
        for i in range(6):
            vec_x[i] = vec_x[i] + size * vec_p[i]
            vec_r[i] = vec_r[i] - size * vec_y[i]
        norm_next = norm()
        ratio = norm_next / norm_now
        for i in range(6):
            vec_p[i] = vec_r[i] + ratio * vec_p[i]
        return norm_next

    lax.fori_loop(0, ITERS, sweep, norm())
    mine = slab * 16 + plane
    for comp in range(3):
        for yl in range(2):
            i = comp * 6 + yl
            out[comp * 2 + yl : comp * 2 + yl + 1, :] = (
                nodes[i : i + 1, :] + vec_x[comp * 2 + yl, pl.ds(mine, 1), :]
            )


def solve_part(place, nodes, pieces):
    vmem = pl.BlockSpec(memory_space=pltpu.VMEM)
    return pl.pallas_call(
        solve_kernel,
        out_shape=jax.ShapeDtypeStruct((6, 128), F32),
        in_specs=[pl.BlockSpec(memory_space=pltpu.SMEM)] + [vmem] * 13,
        out_specs=vmem,
        scratch_shapes=[
            pltpu.VMEM((ROWS * STRIDE, 128), F32),
            pltpu.VMEM((9, 18, 16, 128), F32),
            pltpu.VMEM((18, 16, 128), F32),
        ]
        + [pltpu.VMEM((6, 128, 128), F32)] * 4,
        compiler_params=pltpu.CompilerParams(vmem_limit_bytes=48 << 20),
        name="solve_part",
    )(place, nodes, *pieces)


def coordinates(device):
    slab, plane = divmod(device, 16)
    x, y_hi = divmod(slab, 2)
    z, rest = divmod(plane, 4)
    y_lo, core = divmod(rest, 2)
    return [x, y_hi * 2 + y_lo, z, core]


def device_of(x, y, z, core):
    return (x * 2 + y // 2) * 16 + z * 4 + (y % 2) * 2 + core


def exchange(value, axis, second):
    pairs = []
    for device in range(128):
        at = coordinates(device)
        if axis == 3:
            at[3] = 1 - at[3]
        else:
            at[axis] ^= 3 if (at[3] == 1) != second else 1
        pairs.append((device, device_of(*at)))
    return lax.ppermute(value, AXES, pairs)


def shifted(value, slab_step, plane_step):
    pairs = []
    for slab in range(8 - slab_step):
        for plane in range(16 - plane_step):
            pairs.append((slab * 16 + plane, (slab + slab_step) * 16 + plane + plane_step))
    return lax.ppermute(value, AXES, pairs)


def neighbours(forward, backward, axis):
    count = lax.axis_size(axis)
    up = [(i, i + 1) for i in range(count - 1)]
    down = [(i + 1, i) for i in range(count - 1)]
    return lax.ppermute(forward, axis, up), lax.ppermute(backward, axis, down)


def body(images, shifts, initial_displacement):
    ref, moving = images[0], images[1]
    own_nodes = initial_displacement.reshape(6, 128)

    def wide(rows):
        return jnp.pad(rows.reshape(1, 768), ((0, 0), (0, 256)))

    zlo, zhi = neighbours(
        jnp.concatenate([ref[6:8].reshape(32, 1024), moving[7]], 0),
        jnp.concatenate([ref[0:2].reshape(32, 1024), moving[0], wide(own_nodes)], 0),
        "slab",
    )
    above = zhi[48, :768].reshape(3, 2, 128)
    layers = jnp.stack([initial_displacement[:, 0], above], 1)
    ylo, yhi = neighbours(
        jnp.concatenate(
            [ref[:, 14:16].reshape(16, 1024), zlo[47:48], moving[:, 15], zhi[47:48]], 0
        ),
        jnp.concatenate(
            [
                ref[:, 0:2].reshape(16, 1024),
                zlo[32:33],
                moving[:, 0],
                zhi[32:33],
                wide(layers[:, :, 0]),
            ],
            0,
        ),
        "plane",
    )
    beyond = yhi[26, :768].reshape(3, 2, 1, 128)
    nodes = jnp.concatenate([layers, beyond], 2).reshape(18, 128)
    nodes = jnp.pad(nodes, ((0, 6), (0, 0)))
    elements = jnp.pad(shifts.reshape(6, 128), ((0, 2), (0, 0)))
    mismatch, own, to_slab, to_plane, to_both = local_part(
        images, zlo, zhi, ylo, yhi, elements, nodes
    )
    payload = own + shifted(to_slab, 1, 0) + shifted(to_plane, 0, 1) + shifted(to_both, 1, 1)
    blocks = payload[None]
    for axis in range(3):
        blocks = jnp.concatenate([blocks, exchange(blocks, axis, False)], 0)
    parts = [blocks[:, start : start + count] for start, count in COLORS]
    for turn in range(2):
        parts = [
            jnp.concatenate([part, exchange(part, (color + turn) % 3, True)], 0)
            for color, part in enumerate(parts)
        ]
    last = [exchange(part, (color + 2) % 3, True) for color, part in enumerate(parts)]
    pieces = parts + last
    pieces = pieces + [exchange(piece, 3, False) for piece in pieces]
    place = jnp.stack([lax.axis_index("slab"), lax.axis_index("plane")]).astype(jnp.int32)
    result = solve_part(place, nodes, pieces)
    return result.reshape(3, 1, 2, 128), mismatch


def solution(mesh):
    in_specs = (
        P(None, "slab", "plane", None),
        P(None, "slab", "plane", None),
        P(None, "slab", "plane", None),
    )
    out_specs = (P(None, "slab", "plane", None), P("slab", "plane", None))
    return jax.shard_map(body, mesh=mesh, in_specs=in_specs, out_specs=out_specs, check_vma=False)
```

```python
import jax
import jax.numpy as jnp
import numpy as np
from jax import lax
from jax.experimental import pallas as pl
from jax.experimental.pallas import tpu as pltpu
from jax.sharding import PartitionSpec as P

ELEM = 8
ITERS = 6
reg_weight = 4.0
AXES = ("slab", "plane")
NCHUNK = 8
ROWS = 112
RHS_ROW = 96
U_ROW = 102
ENERGY_ROW = 108
COLORS = ((0, 40), (40, 40), (80, 32))
STRIDE = 136
PAIRS = ((0, 0), (0, 1), (0, 2), (1, 1), (1, 2), (2, 2))
AB = [[0, 1, 2], [1, 3, 4], [2, 4, 5]]
F32 = jnp.float32
BF16 = jnp.bfloat16


def build_constants():
    w = np.arange(8) / 8.0
    lo, up = 1.0 - w, w
    quad = (lo * lo, lo * up, up * up)
    lin = (lo, up)
    wq = np.zeros((1024, 256))
    wl = np.zeros((1024, 128))
    for e in range(128):
        for i in range(8):
            v = 8 * e + i
            wq[v, e] += quad[0][i]
            wq[v, 128 + e] += quad[1][i]
            wl[v, e] += lin[0][i]
            if e + 1 < 128:
                wq[v, e + 1] += quad[2][i]
                wl[v, e + 1] += lin[1][i]
    spread = np.zeros((128, 1024))
    for e in range(128):
        spread[e, 8 * e : 8 * e + 8] = 1.0
    ly = np.zeros((4, 48, 288))
    ry = np.zeros((4, 24, 288))

    def put(which, tz, yk, zt, er, yq):
        for ab in range(6):
            for s in range(8):
                ly[which, (tz * 4 + yk) * 6 + ab, ((zt * 6 + ab) * 2 + er) * 8 + s] += quad[yq][s]

    for which, tz, zt in ((0, 0, 0), (0, 1, 1), (1, 0, 2)):
        put(which, tz, 0, zt, 0, 0)
        put(which, tz, 1, zt, 0, 2)
        put(which, tz, 1, zt, 1, 0)
        put(which, tz, 2, zt, 0, 1)
        put(which, tz, 3, zt, 1, 1)
    for which, tz, zt in ((2, 0, 0), (2, 1, 1), (3, 0, 2)):
        put(which, tz, 0, zt, 1, 2)

    def put_rhs(which, yl, zt, er, yq):
        for c in range(9):
            for s in range(8):
                ry[which, yl * 9 + c, ((zt * 9 + c) * 2 + er) * 8 + s] += lin[yq][s]

    for which, zt in ((0, 0), (1, 1)):
        put_rhs(which, 0, zt, 0, 0)
        put_rhs(which, 1, zt, 0, 1)
        put_rhs(which, 1, zt, 1, 0)
    for which, zt in ((2, 0), (3, 1)):
        put_rhs(which, 0, zt, 1, 1)
    cast = lambda a: jnp.asarray(a.astype(np.float32)).astype(BF16)
    return (
        cast(np.concatenate([wq, wl], 1)),
        cast(np.concatenate([wl.T, spread], 0)),
        cast(np.concatenate([ly.reshape(192, 288), ry.reshape(96, 288)], 0)),
    )


def dot(a, b):
    return lax.dot_general(a, b, (((1,), (0,)), ((), ())), preferred_element_type=F32)


def split_left(a, b, parts=2):
    total = None
    for _ in range(parts):
        piece = a.astype(BF16)
        a = a - piece.astype(F32)
        term = dot(piece, b)
        total = term if total is None else total + term
    return total


def split_right(a, b, parts=2):
    total = None
    for _ in range(parts):
        piece = b.astype(BF16)
        b = b - piece.astype(F32)
        term = dot(a, piece)
        total = term if total is None else total + term
    return total


def by_parity(odd, run, one, two):
    @pl.when(odd == 0)
    def _():
        run(one, two)

    @pl.when(odd == 1)
    def _():
        run(two, one)


def pack_rows_kernel(place, images, nodes, first_send, second_send):
    def fill(last, first):
        for z in range(8):
            last[2 * z : 2 * z + 2, :] = images[0, z, 14:16, :]
            last[16 + z : 17 + z, :] = images[1, z, 15:16, :]
            first[2 * z : 2 * z + 2, :] = images[0, z, 0:2, :]
            first[16 + z : 17 + z, :] = images[1, z, 0:1, :]
        last[24:32, :] = jnp.zeros((8, 1024), F32)
        first[24:32, :] = jnp.zeros((8, 1024), F32)
        for c in range(3):
            first[24:25, 128 * c : 128 * c + 128] = nodes[c, 0, 0:1, :]

    by_parity(place[1] % 2, fill, first_send, second_send)


def pack_planes_kernel(place, images, nodes, first_rows, second_rows, first_send, second_send):
    def fill(forward, backward):
        for target, planes in ((forward, (6, 7, 7)), (backward, (0, 1, 0))):
            target[0:16, :] = images[0, planes[0]]
            target[16:32, :] = images[0, planes[1]]
            target[32:48, :] = images[1, planes[2]]
        forward[48:56, :] = jnp.zeros((8, 1024), F32)
        backward[48:56, :] = jnp.zeros((8, 1024), F32)

        def corners(high, low):
            for target, z in ((forward, 7), (backward, 0)):
                target[48:49, :] = low[16 + z : 17 + z, :]
                target[49:50, :] = high[16 + z : 17 + z, :]
            for c in range(3):
                for y in range(3):
                    i = c * 3 + y
                    source = nodes[c, 0, y : y + 1, :] if y < 2 else high[24:25, 128 * c : 128 * c + 128]
                    at = 128 * (i % 8)
                    backward[50 + i // 8 : 51 + i // 8, at : at + 128] = source

        by_parity(place[1] % 2, corners, first_rows, second_rows)

    by_parity(place[0] % 2, fill, first_send, second_send)


def local_kernel(
    place, images, first_planes, second_planes, first_rows, second_rows, shifts, nodes,
    to_nodes, to_voxels, down_rows,
    mismatch, own, to_slab, to_plane,
    pad0, pad1, gx, sh, un, acc, acc_rhs, near,
):
    lane = lax.broadcasted_iota(jnp.int32, (1, 1024), 1)
    pad0[2:10, 8:24, :] = images[0]
    pad1[1, 1:9, 8:24, :] = images[1]
    near[...] = jnp.zeros((24, 128), F32)
    for c in range(3):
        near[6 * c : 6 * c + 2, :] = nodes[c, 0]

    def put_planes(high, low):
        pad0[0:2, 8:24, :] = low[0:32, :].reshape(2, 16, 1024)
        pad0[10:12, 8:24, :] = high[0:32, :].reshape(2, 16, 1024)
        for k, source in ((0, low), (9, high)):
            pad1[1, k, 8:24, :] = source[32:48, :]
            pad1[1, k, 7:8, :] = source[48:49, :]
            pad1[1, k, 24:25, :] = source[49:50, :]
        for c in range(3):
            for y in range(3):
                i = c * 3 + y
                at = 128 * (i % 8)
                r = 6 * c + 3 + y
                near[r : r + 1, :] = high[50 + i // 8 : 51 + i // 8, at : at + 128]

    def put_rows(high, low):
        for z in range(8):
            pad0[2 + z, 6:8, :] = low[2 * z : 2 * z + 2, :]
            pad0[2 + z, 24:26, :] = high[2 * z : 2 * z + 2, :]
            pad1[1, 1 + z, 7:8, :] = low[16 + z : 17 + z, :]
            pad1[1, 1 + z, 24:25, :] = high[16 + z : 17 + z, :]
        for c in range(3):
            near[6 * c + 2 : 6 * c + 3, :] = high[24:25, 128 * c : 128 * c + 128]

    by_parity(place[0] % 2, put_planes, first_planes, second_planes)
    by_parity(place[1] % 2, put_rows, first_rows, second_rows)

    def lanes(value, off):
        moved = pltpu.roll(value, (-off) % 1024, value.ndim - 1)
        inside = (lane + off >= 0) & (lane + off < 1024)
        return jnp.where(inside, moved, 0.0)

    def shift_planes(k, carry):
        plane = pad1[1, k]
        pad1[0, k] = lanes(plane, -1)
        pad1[2, k] = lanes(plane, 1)
        return carry

    lax.fori_loop(0, 10, shift_planes, 0)

    def along_x(z, carry):
        t = images[0, z]
        gx[z] = (lanes(t, -2) - lanes(t, 2) + 8.0 * (lanes(t, 1) - lanes(t, -1))) * (1.0 / 12.0)
        return carry

    lax.fori_loop(0, 8, along_x, 0)
    for c in range(3):
        sh[2 * c : 2 * c + 2, :] = dot(shifts[c, 0].astype(F32).astype(BF16), to_voxels[128:256, :])
    un[...] = split_left(near[...], to_voxels[0:128, :], 3)
    wy = lax.broadcasted_iota(jnp.int32, (8, 128), 0).astype(F32) * 0.125

    def chunk(c, energy):
        at = pl.ds(pl.multiple_of(c * 128, 128), 128)
        for er in range(2):
            base = 8 + 8 * er

            def full(row):
                return jnp.broadcast_to(row, (8, 128))

            sz = full(sh[er : er + 1, at])
            sy = full(sh[2 + er : 3 + er, at])
            sx = full(sh[4 + er : 5 + er, at])
            x_low, x_up = sx < -0.5, sx > 0.5
            y_low, y_up = sy < -0.5, sy > 0.5
            z_low, z_up = sz < -0.5, sz > 0.5

            def in_plane(k):
                rows = []
                for dy in (-1, 0, 1):
                    a, b, d = (pad1[i, k, base + dy : base + dy + 8, at] for i in range(3))
                    rows.append(jnp.where(x_low, a, jnp.where(x_up, d, b)))
                return jnp.where(y_low, rows[0], jnp.where(y_up, rows[2], rows[1]))

            corner = []
            for comp in range(3):
                for zn in range(2):
                    i = (comp * 2 + zn) * 3 + er
                    first, second = full(un[i : i + 1, at]), full(un[i + 1 : i + 2, at])
                    corner.append(first + wy * (second - first))
            sums = [None] * 18
            sums_rhs = [None] * 6
            planes = [in_plane(0), in_plane(1)]
            for z in range(8):
                planes.append(in_plane(z + 2))
                warped = jnp.where(z_low, planes[z], jnp.where(z_up, planes[z + 2], planes[z + 1]))
                here = lambda k: pad0[k, base : base + 8, at]
                rows = lambda dy: pad0[z + 2, base + dy : base + dy + 8, at]
                g0 = (here(z) - here(z + 4) + 8.0 * (here(z + 3) - here(z + 1))) * (1.0 / 12.0)
                g1 = (rows(-2) - rows(2) + 8.0 * (rows(1) - rows(-1))) * (1.0 / 12.0)
                g2 = gx[z, base - 8 : base, at]
                g = (g0, g1, g2)
                w = z / 8.0
                total = None
                for comp in range(3):
                    moved = corner[2 * comp] + w * (corner[2 * comp + 1] - corner[2 * comp])
                    term = g[comp] * moved
                    total = term if total is None else total + term
                mis = here(z + 2) - warped - total
                mismatch[z, base - 8 : base, at] = mis

                def add(store, i, weight, value):
                    if weight:
                        term = value if weight == 1.0 else weight * value
                        store[i] = term if store[i] is None else store[i] + term

                for ab, (a, b) in enumerate(PAIRS):
                    prod = g[a] * g[b]
                    if a == b:
                        energy = energy + prod
                    for zt, weight in enumerate(((1 - w) * (1 - w), w * (1 - w), w * w)):
                        add(sums, zt * 6 + ab, weight, prod)
                for comp in range(3):
                    prod = g[comp] * mis
                    for zt, weight in enumerate((1 - w, w)):
                        add(sums_rhs, zt * 3 + comp, weight, prod)
            for i in range(18):
                r = (i * 2 + er) * 8
                acc[r : r + 8, at] = sums[i]
            for zt in range(2):
                for c in range(9):
                    r = ((zt * 9 + c) * 2 + er) * 8
                    if c < 3:
                        value = sums_rhs[zt * 3 + c]
                    else:
                        value = sums[zt * 6 + c - 3] + sums[zt * 6 + c + 3]
                    acc_rhs[r : r + 8, at] = value
        return energy

    energy = lax.fori_loop(0, NCHUNK, chunk, jnp.zeros((8, 128), F32))
    by_x = split_left(acc[...], to_nodes[:, 0:256])
    by_x_rhs = split_left(acc_rhs[...], to_nodes[:, 256:384])
    by_y = split_right(down_rows[0:192, :], by_x)
    by_y_rhs = split_right(down_rows[192:288, :], by_x_rhs)
    def edges(which, tx, first, count):
        r = 48 * which + first
        return by_y[r : r + count, 128 * tx : 128 * tx + 128]

    def whole(which, yl):
        r = 24 * which + 9 * yl
        return by_y_rhs[r + 3 : r + 9, :]

    def load(which, yl):
        r = 24 * which + 9 * yl
        return by_y_rhs[r : r + 3, :]

    own[0:6, :] = whole(0, 0)
    own[6:12, :] = whole(0, 1)
    own[12:48, :] = edges(0, 0, 12, 36)
    own[48:96, :] = edges(0, 1, 0, 48)
    own[96:99, :] = load(0, 0)
    own[99:102, :] = load(0, 1)
    own[108:112, :] = jnp.zeros((4, 128), F32)
    to_slab[0:6, :] = whole(1, 0)
    to_slab[6:12, :] = whole(1, 1)
    to_slab[12:24, :] = edges(1, 0, 12, 12)
    to_slab[24:48, :] = edges(1, 1, 0, 24)
    to_slab[48:51, :] = load(1, 0)
    to_slab[51:54, :] = load(1, 1)
    to_slab[54:56, :] = jnp.zeros((2, 128), F32)
    to_plane[0:6, :] = whole(2, 0)
    to_plane[6:12, :] = edges(2, 0, 24, 6)
    to_plane[12:18, :] = edges(2, 1, 0, 6)
    to_plane[18:24, :] = edges(2, 1, 24, 6)
    to_plane[24:30, :] = whole(3, 0)
    to_plane[30:36, :] = edges(3, 1, 0, 6)
    to_plane[36:39, :] = load(2, 0)
    to_plane[39:42, :] = load(3, 0)
    to_plane[42:48, :] = jnp.zeros((6, 128), F32)
    for yl in range(2):
        for comp in range(3):
            r = U_ROW + yl * 3 + comp
            own[r : r + 1, :] = nodes[comp, 0, yl : yl + 1, :]
    own[ENERGY_ROW : ENERGY_ROW + 1, :] = jnp.sum(energy, axis=0, keepdims=True)


VMEM = pl.BlockSpec(memory_space=pltpu.VMEM)
SMEM = pl.BlockSpec(memory_space=pltpu.SMEM)


def pack(kernel, name, rows, place, *arrays):
    shape = jax.ShapeDtypeStruct((rows, 1024), F32)
    return pl.pallas_call(
        kernel,
        out_shape=(shape, shape),
        in_specs=[SMEM] + [VMEM] * len(arrays),
        out_specs=(VMEM, VMEM),
        compiler_params=pltpu.CompilerParams(vmem_limit_bytes=6 << 20),
        name=name,
    )(place, *arrays)


def local_part(place, *arrays):
    message = lambda rows: jax.ShapeDtypeStruct((rows, 128), F32)
    constants = build_constants()
    return pl.pallas_call(
        local_kernel,
        out_shape=(
            jax.ShapeDtypeStruct((8, 16, 1024), F32), message(ROWS), message(56), message(48)
        ),
        in_specs=[SMEM] + [VMEM] * 10,
        out_specs=(VMEM,) * 4,
        scratch_shapes=[
            pltpu.VMEM((12, 32, 1024), F32),
            pltpu.VMEM((3, 10, 32, 1024), F32),
            pltpu.VMEM((8, 16, 1024), F32),
            pltpu.VMEM((8, 1024), F32),
            pltpu.VMEM((24, 1024), F32),
            pltpu.VMEM((288, 1024), F32),
            pltpu.VMEM((288, 1024), F32),
            pltpu.VMEM((24, 128), F32),
        ],
        compiler_params=pltpu.CompilerParams(vmem_limit_bytes=18 << 20),
        name="local_part",
    )(place, *arrays, *constants)


def solve_kernel(*refs):
    place, nodes = refs[0], refs[1]
    pieces = refs[2:14]
    out = refs[14]
    data, var, high, next_row, vec_x, vec_r, vec_p, vec_y = refs[15:]
    slab, plane = place[0], place[1]
    x_me, y_me = slab // 2, (slab % 2) * 2 + (plane // 2) % 2
    z_me, core = plane // 4, plane % 2

    def arrange(j, carry):
        for source in range(2):
            k = core if source == 0 else 1 - core
            first, second = 3 - 2 * k, 1 + 2 * k
            bits = [(j >> i) & 1 for i in range(5)]
            for color in range(3):
                start, count = COLORS[color]
                order = [(color + i) % 3 for i in range(3)]
                for half in range(2):
                    delta = [bits[0] * first, bits[1] * first, bits[2] * first]
                    delta[order[0]] = delta[order[0]] ^ (bits[3] * second)
                    delta[order[1]] = delta[order[1]] ^ (bits[4] * second)
                    if half:
                        delta[order[2]] = delta[order[2]] ^ second
                    x, y, z = x_me ^ delta[0], y_me ^ delta[1], z_me ^ delta[2]
                    device = (x * 2 + (y >> 1)) * 16 + z * 4 + (y & 1) * 2 + k
                    piece = pieces[(source * 2 + half) * 3 + color]
                    for t in range(count // 8):
                        r = (start + 8 * t) * STRIDE
                        data[pl.ds(r + device, 8, stride=STRIDE), :] = piece[j, 8 * t : 8 * t + 8, :]
        return carry

    lax.fori_loop(0, 32, arrange, 0)

    def field(r):
        return data[r * STRIDE : r * STRIDE + 128, :]

    total = jnp.sum(jnp.sum(field(ENERGY_ROW), axis=0, keepdims=True), axis=1, keepdims=True)
    penalty = reg_weight / (64.0 * 256.0 * 1024.0) * total

    def row_of(tx, tz, yk, ab):
        return ((tx * 2 + tz) * 4 + yk) * 6 + ab

    lane = lax.broadcasted_iota(jnp.int32, (128, 128), 1)
    row = lax.broadcasted_iota(jnp.int32, (128, 128), 0)
    in_plane = row % 16
    first = (lane == 0).astype(F32) + (row < 16).astype(F32)
    first = (first, first)
    first = (first[0] + (in_plane == 0).astype(F32), first[1])
    for ab in (0, 3, 5):
        for yl in range(2):
            for tx, tz, yk, weight in (
                (0, 0, yl, first[yl]), (0, 0, 2 + yl, -1.0), (0, 1, yl, -1.0), (1, 0, yl, -1.0)
            ):
                r = row_of(tx, tz, yk, ab) * STRIDE
                data[r : r + 128, :] = data[r : r + 128, :] + weight * penalty

    def x_next(v):
        return jnp.where(lane < 127, pltpu.roll(v, 127, 1), 0.0)

    def x_prev(v):
        return jnp.where(lane > 0, pltpu.roll(v, 1, 1), 0.0)

    def p_next(v):
        return jnp.where(in_plane < 15, pltpu.roll(v, 127, 0), 0.0)

    def p_prev(v):
        return jnp.where(in_plane > 0, pltpu.roll(v, 1, 0), 0.0)

    zero = jnp.zeros((16, 128), F32)

    def z_next(v):
        return jnp.concatenate([v[16:], zero], axis=0)

    def z_prev(v):
        return jnp.concatenate([zero, v[:112]], axis=0)

    for comp in range(3):
        u = [field(U_ROW + yl * 3 + comp) for yl in range(2)]
        for yl in range(2):
            v = u[yl]
            beside = z_next(v) + z_prev(v) + x_next(v) + x_prev(v)
            beside = beside + (u[1] + p_prev(u[1]) if yl == 0 else u[0] + p_next(u[0]))
            rhs = field(RHS_ROW + yl * 3 + comp) - penalty * (6.0 * v - beside)
            i = comp * 2 + yl
            vec_r[i] = rhs
            vec_p[i] = rhs
            vec_x[i] = jnp.zeros((128, 128), F32)

    def norm():
        value = None
        for i in range(6):
            term = vec_r[i] * vec_r[i]
            value = term if value is None else value + term
        return jnp.sum(jnp.sum(value, axis=0, keepdims=True), axis=1, keepdims=True)

    var[:, 128:144, :] = jnp.zeros((18, 16, 128), F32)
    lane8 = lax.broadcasted_iota(jnp.int32, (8, 128), 1)
    Y_CORNERS = ((0,), (1,), (0, 1), (1, 2))

    def multiply(i, carry):
        here = pl.ds(pl.multiple_of(i * 8, 8), 8)
        above = pl.ds(pl.multiple_of(i * 8 + 16, 8), 8)
        held = (i % 2) * 18
        values = {}
        for z in range(2):
            for b in range(3):
                for y in range(3):
                    for x in range(2):
                        k = (b * 3 + y) * 2 + x
                        values[z, y, x, b] = var[k, above if z else here, :]
        sums = {}

        def add(corner, a, value, sign=1):
            z, y, x = corner
            key = (z, y, x, a)
            if key not in sums:
                sums[key] = high[held + 3 * (y * 2 + x) + a] if z == 0 else None
            old = sums[key]
            if old is None:
                sums[key] = value if sign > 0 else -value
            else:
                sums[key] = old + value if sign > 0 else old - value

        def product(tx, tz, yk, v):
            m = []
            for ab in range(6):
                start = row_of(tx, tz, yk, ab) * STRIDE
                m.append(data[pl.ds(pl.multiple_of(start + i * 8, 8), 8), :])
            return [m[AB[a][0]] * v[0] + m[AB[a][1]] * v[1] + m[AB[a][2]] * v[2] for a in range(3)]

        for tz in range(2):
            for tx in range(2):
                for yk in range(4):
                    ys = Y_CORNERS[yk]
                    if tz == 0 and tx == 0 and yk < 2:
                        v = [values[0, ys[0], 0, b] for b in range(3)]
                        for a, q in enumerate(product(tx, tz, yk, v)):
                            add((0, ys[0], 0), a, q)
                        continue
                    ends = []
                    for oz in range(1 + tz):
                        for oy in range(len(ys)):
                            for ox in range(1 + tx):
                                one = (oz, ys[oy], ox)
                                two = (tz - oz, ys[len(ys) - 1 - oy], tx - ox)
                                if (two, one) not in ends:
                                    ends.append((one, two))
                    for one, two in ends:
                        v = [values[two + (b,)] - values[one + (b,)] for b in range(3)]
                        for a, q in enumerate(product(tx, tz, yk, v)):
                            add(one, a, q)
                            add(two, a, q, -1)
        for a in range(3):
            for y in range(3):
                part = sums[0, y, 0, a] + jnp.where(
                    lane8 > 0, pltpu.roll(sums[0, y, 1, a], 1, 1), 0.0
                )
                if y < 2:
                    vec_y[a * 2 + y, here, :] = part
                else:
                    next_row[a, here, :] = part
                for x in range(2):
                    high[held + 3 * (y * 2 + x) + a] = sums[1, y, x, a]
        return carry

    def sweep(step, norm_now):
        for comp in range(3):
            own = [vec_p[comp * 2 + yl] for yl in range(2)]
            for y_kind, v in enumerate((own[0], own[1], p_next(own[0]))):
                i = (comp * 3 + y_kind) * 2
                var[i, 0:128, :] = v
                var[i + 1, 0:128, :] = x_next(v)
        high[...] = jnp.zeros((36, 8, 128), F32)
        lax.fori_loop(0, 16, multiply, 0)
        energy = None
        for comp in range(3):
            vec_y[comp * 2] = vec_y[comp * 2] + p_prev(next_row[comp])
            for yl in range(2):
                term = vec_y[comp * 2 + yl] * vec_p[comp * 2 + yl]
                energy = term if energy is None else energy + term
        curvature = jnp.sum(jnp.sum(energy, axis=0, keepdims=True), axis=1, keepdims=True)
        size = norm_now / curvature
        for i in range(6):
            vec_x[i] = vec_x[i] + size * vec_p[i]
            vec_r[i] = vec_r[i] - size * vec_y[i]
        norm_next = norm()
        ratio = norm_next / norm_now
        for i in range(6):
            vec_p[i] = vec_r[i] + ratio * vec_p[i]
        return norm_next

    lax.fori_loop(0, ITERS, sweep, norm())
    mine = slab * 16 + plane
    for comp in range(3):
        for yl in range(2):
            out[comp, 0, yl : yl + 1, :] = (
                nodes[comp, 0, yl : yl + 1, :] + vec_x[comp * 2 + yl, pl.ds(mine, 1), :]
            )


def solve_part(place, nodes, pieces):
    return pl.pallas_call(
        solve_kernel,
        out_shape=jax.ShapeDtypeStruct((3, 1, 2, 128), F32),
        in_specs=[SMEM] + [VMEM] * 13,
        out_specs=VMEM,
        scratch_shapes=[
            pltpu.VMEM((ROWS * STRIDE, 128), F32),
            pltpu.VMEM((18, 144, 128), F32),
            pltpu.VMEM((36, 8, 128), F32),
            pltpu.VMEM((3, 128, 128), F32),
        ]
        + [pltpu.VMEM((6, 128, 128), F32)] * 4,
        compiler_params=pltpu.CompilerParams(vmem_limit_bytes=18 << 20),
        name="solve_part",
    )(place, nodes, *pieces)


def coordinates(device):
    slab, plane = divmod(device, 16)
    x, y_hi = divmod(slab, 2)
    z, rest = divmod(plane, 4)
    y_lo, core = divmod(rest, 2)
    return [x, y_hi * 2 + y_lo, z, core]


def device_of(x, y, z, core):
    return (x * 2 + y // 2) * 16 + z * 4 + (y % 2) * 2 + core


def exchange(value, axis, second):
    pairs = []
    for device in range(128):
        at = coordinates(device)
        if axis == 3:
            at[3] = 1 - at[3]
        else:
            at[axis] ^= 3 if (at[3] == 1) == second else 1
        pairs.append((device, device_of(*at)))
    return lax.ppermute(value, AXES, pairs)


def shifted(value, slab_step, plane_step):
    pairs = []
    for slab in range(8 - slab_step):
        for plane in range(16 - plane_step):
            pairs.append((slab * 16 + plane, (slab + slab_step) * 16 + plane + plane_step))
    return lax.ppermute(value, AXES, pairs)


def swap(value, axis, second):
    count = lax.axis_size(axis)
    pairs = []
    for i in range(count):
        j = i + (1 if (i % 2 == 1) == second else -1)
        if 0 <= j < count:
            pairs.append((i, j))
    return lax.ppermute(value, axis, pairs)


def body(images, shifts, nodes):
    place = jnp.stack([lax.axis_index("slab"), lax.axis_index("plane")]).astype(jnp.int32)
    first, second = pack(pack_rows_kernel, "pack_rows", 32, place, images, nodes)
    rows = swap(first, "plane", False), swap(second, "plane", True)
    first, second = pack(pack_planes_kernel, "pack_planes", 56, place, images, nodes, *rows)
    planes = swap(first, "slab", False), swap(second, "slab", True)
    mismatch, own, to_slab, to_plane = local_part(place, images, *planes, *rows, shifts, nodes)

    def spaced(value, layout):
        rows = []
        for start, count, gap in layout:
            rows += [value[start : start + count], jnp.zeros((gap, 128), F32)]
        return jnp.concatenate(rows, 0)

    got = shifted(to_plane, 0, 1)
    to_slab = to_slab + spaced(got, ((24, 6, 18), (30, 6, 18), (39, 3, 5)))
    own = own + spaced(got, ((0, 6, 18), (6, 6, 18), (12, 6, 18), (18, 6, 18), (36, 3, 13)))
    got = shifted(to_slab, 1, 0)
    payload = own + spaced(got, ((0, 24, 24), (24, 24, 24), (48, 6, 10)))
    blocks = payload[None]
    for axis in range(3):
        blocks = jnp.concatenate([blocks, exchange(blocks, axis, False)], 0)
    parts = [blocks[:, start : start + count] for start, count in COLORS]
    for turn in range(2):
        parts = [
            jnp.concatenate([part, exchange(part, (color + turn) % 3, True)], 0)
            for color, part in enumerate(parts)
        ]
        parts = list(lax.optimization_barrier(tuple(parts)))
    last = [exchange(part, (color + 2) % 3, True) for color, part in enumerate(parts)]
    pieces = parts + last
    pieces = pieces + [exchange(piece, 3, False) for piece in pieces]
    result = solve_part(place, nodes, pieces)
    return result, mismatch


def solution(mesh):
    in_specs = (
        P(None, "slab", "plane", None),
        P(None, "slab", "plane", None),
        P(None, "slab", "plane", None),
    )
    out_specs = (P(None, "slab", "plane", None), P("slab", "plane", None))
    return jax.shard_map(body, mesh=mesh, in_specs=in_specs, out_specs=out_specs, check_vma=False)
```

```python
import jax
import jax.numpy as jnp
import numpy as np
from jax import lax
from jax.experimental import pallas as pl
from jax.experimental.pallas import tpu as pltpu
from jax.sharding import PartitionSpec as P


ITERS = 6
reg_weight = 4.0
AXES = ("slab", "plane")
NCHUNK = 8
ROWS = 112
RHS_ROW = 96
U_ROW = 102
ENERGY_ROW = 108
COLORS = ((0, 40), (40, 40), (80, 32))
STRIDE = 136
LIMIT_A = 2 << 20
LIMIT_B = 9 << 20
PAIRS = ((0, 0), (0, 1), (0, 2), (1, 1), (1, 2), (2, 2))
AB = [[0, 1, 2], [1, 3, 4], [2, 4, 5]]
F32 = jnp.float32
BF16 = jnp.bfloat16


def build_constants():
    w = np.arange(8) / 8.0
    lo, up = 1.0 - w, w
    quad = (lo * lo, lo * up, up * up)
    lin = (lo, up)
    wq = np.zeros((1024, 256))
    wl = np.zeros((1024, 128))
    for e in range(128):
        for i in range(8):
            v = 8 * e + i
            wq[v, e] += quad[0][i]
            wq[v, 128 + e] += quad[1][i]
            wl[v, e] += lin[0][i]
            if e + 1 < 128:
                wq[v, e + 1] += quad[2][i]
                wl[v, e + 1] += lin[1][i]
    spread = np.zeros((128, 1024))
    for e in range(128):
        spread[e, 8 * e : 8 * e + 8] = 1.0
    ly = np.zeros((4, 48, 288))
    ry = np.zeros((4, 24, 288))

    def put(which, tz, yk, zt, er, yq):
        for ab in range(6):
            for s in range(8):
                ly[which, (tz * 4 + yk) * 6 + ab, ((zt * 6 + ab) * 2 + er) * 8 + s] += quad[yq][s]

    for which, tz, zt in ((0, 0, 0), (0, 1, 1), (1, 0, 2)):
        put(which, tz, 0, zt, 0, 0)
        put(which, tz, 1, zt, 0, 2)
        put(which, tz, 1, zt, 1, 0)
        put(which, tz, 2, zt, 0, 1)
        put(which, tz, 3, zt, 1, 1)
    for which, tz, zt in ((2, 0, 0), (2, 1, 1), (3, 0, 2)):
        put(which, tz, 0, zt, 1, 2)

    def put_rhs(which, yl, zt, er, yq):
        for c in range(9):
            for s in range(8):
                ry[which, yl * 9 + c, ((zt * 9 + c) * 2 + er) * 8 + s] += lin[yq][s]

    for which, zt in ((0, 0), (1, 1)):
        put_rhs(which, 0, zt, 0, 0)
        put_rhs(which, 1, zt, 0, 1)
        put_rhs(which, 1, zt, 1, 0)
    for which, zt in ((2, 0), (3, 1)):
        put_rhs(which, 0, zt, 1, 1)
    cast = lambda a: jnp.asarray(a.astype(np.float32)).astype(BF16)
    return (
        cast(np.concatenate([wq, wl], 1)),
        cast(np.concatenate([wl.T, spread], 0)),
        cast(np.concatenate([ly.reshape(192, 288), ry.reshape(96, 288)], 0)),
    )


def dot(a, b):
    return lax.dot_general(a, b, (((1,), (0,)), ((), ())), preferred_element_type=F32)


def split_left(a, b, parts=2):
    total = None
    for _ in range(parts):
        piece = a.astype(BF16)
        a = a - piece.astype(F32)
        term = dot(piece, b)
        total = term if total is None else total + term
    return total


def split_right(a, b, parts=2):
    total = None
    for _ in range(parts):
        piece = b.astype(BF16)
        b = b - piece.astype(F32)
        term = dot(a, piece)
        total = term if total is None else total + term
    return total


def by_parity(odd, run, one, two):
    @pl.when(odd == 0)
    def _():
        run(one, two)

    @pl.when(odd == 1)
    def _():
        run(two, one)


def pack_rows_kernel(place, images_in, nodes_in, first_send, second_send, images, nodes, sems):
    copies = [pltpu.make_async_copy(nodes_in, nodes, sems.at[4])]
    for i in range(2):
        for k in range(2):
            part = (i, pl.ds(4 * k, 4))
            copies.append(
                pltpu.make_async_copy(images_in.at[part], images.at[part], sems.at[2 * i + k])
            )
    for copy in copies:
        copy.start()
    for copy in copies:
        copy.wait()

    def fill(last, first):
        for z in range(8):
            last[2 * z : 2 * z + 2, :] = images[0, z, 14:16, :]
            last[16 + z : 17 + z, :] = images[1, z, 15:16, :]
            first[2 * z : 2 * z + 2, :] = images[0, z, 0:2, :]
            first[16 + z : 17 + z, :] = images[1, z, 0:1, :]
        last[24:32, :] = jnp.zeros((8, 1024), F32)
        first[24:32, :] = jnp.zeros((8, 1024), F32)
        for c in range(3):
            first[24:25, 128 * c : 128 * c + 128] = nodes[c, 0, 0:1, :]

    by_parity(place[1] % 2, fill, first_send, second_send)


def pack_planes_kernel(place, images, nodes, first_rows, second_rows, first_send, second_send):
    def fill(forward, backward):
        for target, planes in ((forward, (6, 7, 7)), (backward, (0, 1, 0))):
            target[0:16, :] = images[0, planes[0]]
            target[16:32, :] = images[0, planes[1]]
            target[32:48, :] = images[1, planes[2]]
        forward[48:56, :] = jnp.zeros((8, 1024), F32)
        backward[48:56, :] = jnp.zeros((8, 1024), F32)

        def corners(high, low):
            for target, z in ((forward, 7), (backward, 0)):
                target[48:49, :] = low[16 + z : 17 + z, :]
                target[49:50, :] = high[16 + z : 17 + z, :]
            for c in range(3):
                for y in range(3):
                    i = c * 3 + y
                    source = nodes[c, 0, y : y + 1, :] if y < 2 else high[24:25, 128 * c : 128 * c + 128]
                    at = 128 * (i % 8)
                    backward[50 + i // 8 : 51 + i // 8, at : at + 128] = source

        by_parity(place[1] % 2, corners, first_rows, second_rows)

    by_parity(place[0] % 2, fill, first_send, second_send)


def shift_lanes(value, off):
    lane = lax.broadcasted_iota(jnp.int32, (1, 1024), 1)
    moved = pltpu.roll(value, (-off) % 1024, value.ndim - 1)
    inside = (lane + off >= 0) & (lane + off < 1024)
    return jnp.where(inside, moved, 0.0)


def inner_kernel(place, images, first_rows, second_rows, mid0, mid1, gx):
    mid0[:, 8:24, :] = images[0]
    mid1[1, :, 8:24, :] = images[1]

    def put_rows(high, low):
        for z in range(8):
            mid0[z, 6:8, :] = low[2 * z : 2 * z + 2, :]
            mid0[z, 24:26, :] = high[2 * z : 2 * z + 2, :]
            mid1[1, z, 7:8, :] = low[16 + z : 17 + z, :]
            mid1[1, z, 24:25, :] = high[16 + z : 17 + z, :]

    by_parity(place[1] % 2, put_rows, first_rows, second_rows)

    def along_x(z, carry):
        plane = mid1[1, z]
        mid1[0, z] = shift_lanes(plane, -1)
        mid1[2, z] = shift_lanes(plane, 1)
        t = images[0, z]
        near = shift_lanes(t, 1) - shift_lanes(t, -1)
        gx[z] = (shift_lanes(t, -2) - shift_lanes(t, 2) + 8.0 * near) * (1.0 / 12.0)
        return carry

    lax.fori_loop(0, 8, along_x, 0)


def inner_part(place, images, *rows):
    return pl.pallas_call(
        inner_kernel,
        out_shape=(
            jax.ShapeDtypeStruct((8, 32, 1024), F32),
            jax.ShapeDtypeStruct((3, 8, 32, 1024), F32),
            jax.ShapeDtypeStruct((8, 16, 1024), F32),
        ),
        in_specs=[SMEM] + [VMEM] * 3,
        out_specs=(VMEM,) * 3,
        compiler_params=pltpu.CompilerParams(vmem_limit_bytes=8 << 20),
        name="inner_part",
    )(place, images, *rows)


def local_kernel(
    place, mid0, mid1, gx, first_planes, second_planes, first_rows, second_rows, nodes,
    shifts_in, to_nodes_in, to_voxels_in, down_rows_in,
    mismatch, own, to_slab, to_plane,
    out0, out1, sh, un, acc, acc_rhs, near, shifts, to_nodes, to_voxels, down_rows, sems,
):
    pairs = (
        (shifts_in, shifts), (to_voxels_in, to_voxels), (to_nodes_in, to_nodes),
        (down_rows_in, down_rows),
    )
    copies = [pltpu.make_async_copy(a, b, sems.at[i]) for i, (a, b) in enumerate(pairs)]
    for copy in copies:
        copy.start()
    near[...] = jnp.zeros((24, 128), F32)
    for c in range(3):
        near[6 * c : 6 * c + 2, :] = nodes[c, 0]

    def put_planes(high, low):
        out0[0:2] = low[0:32, :].reshape(2, 16, 1024)
        out0[2:4] = high[0:32, :].reshape(2, 16, 1024)
        for k, source in ((0, low), (1, high)):
            out1[1, k, 8:24, :] = source[32:48, :]
            out1[1, k, 7:8, :] = source[48:49, :]
            out1[1, k, 24:25, :] = source[49:50, :]
        for c in range(3):
            for y in range(3):
                i = c * 3 + y
                at = 128 * (i % 8)
                r = 6 * c + 3 + y
                near[r : r + 1, :] = high[50 + i // 8 : 51 + i // 8, at : at + 128]

    def put_rows(high, low):
        for c in range(3):
            near[6 * c + 2 : 6 * c + 3, :] = high[24:25, 128 * c : 128 * c + 128]

    by_parity(place[0] % 2, put_planes, first_planes, second_planes)
    by_parity(place[1] % 2, put_rows, first_rows, second_rows)
    for k in range(2):
        plane = out1[1, k]
        out1[0, k] = shift_lanes(plane, -1)
        out1[2, k] = shift_lanes(plane, 1)
    copies[0].wait()
    copies[1].wait()
    for c in range(3):
        sh[2 * c : 2 * c + 2, :] = dot(shifts[c, 0].astype(F32).astype(BF16), to_voxels[128:256, :])
    un[...] = split_left(near[...], to_voxels[0:128, :], 3)
    wy = lax.broadcasted_iota(jnp.int32, (8, 128), 0).astype(F32) * 0.125

    def chunk(c, energy):
        at = pl.ds(pl.multiple_of(c * 128, 128), 128)
        for er in range(2):
            base = 8 + 8 * er

            def full(row):
                return jnp.broadcast_to(row, (8, 128))

            sz = full(sh[er : er + 1, at])
            sy = full(sh[2 + er : 3 + er, at])
            sx = full(sh[4 + er : 5 + er, at])
            x_low, x_up = sx < -0.5, sx > 0.5
            y_low, y_up = sy < -0.5, sy > 0.5
            z_low, z_up = sz < -0.5, sz > 0.5

            def in_plane(k):
                rows = []
                for dy in (-1, 0, 1):
                    ref, i = (mid1, k - 1) if 1 <= k <= 8 else (out1, k // 9)
                    a, b, d = (ref[n, i, base + dy : base + dy + 8, at] for n in range(3))
                    rows.append(jnp.where(x_low, a, jnp.where(x_up, d, b)))
                return jnp.where(y_low, rows[0], jnp.where(y_up, rows[2], rows[1]))

            corner = []
            for comp in range(3):
                for zn in range(2):
                    i = (comp * 2 + zn) * 3 + er
                    first, second = full(un[i : i + 1, at]), full(un[i + 1 : i + 2, at])
                    corner.append(first + wy * (second - first))
            sums = [None] * 18
            sums_rhs = [None] * 6
            planes = [in_plane(0), in_plane(1)]
            for z in range(8):
                planes.append(in_plane(z + 2))
                warped = jnp.where(z_low, planes[z], jnp.where(z_up, planes[z + 2], planes[z + 1]))

                def here(k):
                    if 2 <= k <= 9:
                        return mid0[k - 2, base : base + 8, at]
                    return out0[k if k < 2 else k - 8, base - 8 : base, at]

                rows = lambda dy: mid0[z, base + dy : base + dy + 8, at]
                g0 = (here(z) - here(z + 4) + 8.0 * (here(z + 3) - here(z + 1))) * (1.0 / 12.0)
                g1 = (rows(-2) - rows(2) + 8.0 * (rows(1) - rows(-1))) * (1.0 / 12.0)
                g2 = gx[z, base - 8 : base, at]
                g = (g0, g1, g2)
                w = z / 8.0
                total = None
                for comp in range(3):
                    moved = corner[2 * comp] + w * (corner[2 * comp + 1] - corner[2 * comp])
                    term = g[comp] * moved
                    total = term if total is None else total + term
                mis = here(z + 2) - warped - total
                mismatch[z, base - 8 : base, at] = mis

                def add(store, i, weight, value):
                    if weight:
                        term = value if weight == 1.0 else weight * value
                        store[i] = term if store[i] is None else store[i] + term

                for ab, (a, b) in enumerate(PAIRS):
                    prod = g[a] * g[b]
                    if a == b:
                        energy = energy + prod
                    for zt, weight in enumerate(((1 - w) * (1 - w), w * (1 - w), w * w)):
                        add(sums, zt * 6 + ab, weight, prod)
                for comp in range(3):
                    prod = g[comp] * mis
                    for zt, weight in enumerate((1 - w, w)):
                        add(sums_rhs, zt * 3 + comp, weight, prod)
            for i in range(18):
                r = (i * 2 + er) * 8
                acc[r : r + 8, at] = sums[i]
            for zt in range(2):
                for c in range(9):
                    r = ((zt * 9 + c) * 2 + er) * 8
                    if c < 3:
                        value = sums_rhs[zt * 3 + c]
                    else:
                        value = sums[zt * 6 + c - 3] + sums[zt * 6 + c + 3]
                    acc_rhs[r : r + 8, at] = value
        return energy

    energy = lax.fori_loop(0, NCHUNK, chunk, jnp.zeros((8, 128), F32))
    copies[2].wait()
    copies[3].wait()
    by_x = split_left(acc[...], to_nodes[:, 0:256])
    by_x_rhs = split_left(acc_rhs[...], to_nodes[:, 256:384])
    by_y = split_right(down_rows[0:192, :], by_x)
    by_y_rhs = split_right(down_rows[192:288, :], by_x_rhs)

    def edges(which, tx, first, count):
        r = 48 * which + first
        return by_y[r : r + count, 128 * tx : 128 * tx + 128]

    def whole(which, yl):
        r = 24 * which + 9 * yl
        return by_y_rhs[r + 3 : r + 9, :]

    def load(which, yl):
        r = 24 * which + 9 * yl
        return by_y_rhs[r : r + 3, :]

    own[0:6, :] = whole(0, 0)
    own[6:12, :] = whole(0, 1)
    own[12:48, :] = edges(0, 0, 12, 36)
    own[48:96, :] = edges(0, 1, 0, 48)
    own[96:99, :] = load(0, 0)
    own[99:102, :] = load(0, 1)
    own[108:112, :] = jnp.zeros((4, 128), F32)
    to_slab[0:6, :] = whole(1, 0)
    to_slab[6:12, :] = whole(1, 1)
    to_slab[12:24, :] = edges(1, 0, 12, 12)
    to_slab[24:48, :] = edges(1, 1, 0, 24)
    to_slab[48:51, :] = load(1, 0)
    to_slab[51:54, :] = load(1, 1)
    to_slab[54:56, :] = jnp.zeros((2, 128), F32)
    to_plane[0:6, :] = whole(2, 0)
    to_plane[6:12, :] = edges(2, 0, 24, 6)
    to_plane[12:18, :] = edges(2, 1, 0, 6)
    to_plane[18:24, :] = edges(2, 1, 24, 6)
    to_plane[24:30, :] = whole(3, 0)
    to_plane[30:36, :] = edges(3, 1, 0, 6)
    to_plane[36:39, :] = load(2, 0)
    to_plane[39:42, :] = load(3, 0)
    to_plane[42:48, :] = jnp.zeros((6, 128), F32)
    for yl in range(2):
        for comp in range(3):
            r = U_ROW + yl * 3 + comp
            own[r : r + 1, :] = nodes[comp, 0, yl : yl + 1, :]
    own[ENERGY_ROW : ENERGY_ROW + 1, :] = jnp.sum(energy, axis=0, keepdims=True)


VMEM = pl.BlockSpec(memory_space=pltpu.VMEM)
SMEM = pl.BlockSpec(memory_space=pltpu.SMEM)
HBM = pl.BlockSpec(memory_space=pltpu.HBM)


def in_hbm(array):
    return pltpu.with_memory_space_constraint(array, pltpu.HBM)


def pack_rows(place, images, nodes):
    message = jax.ShapeDtypeStruct((32, 1024), F32)
    return pl.pallas_call(
        pack_rows_kernel,
        out_shape=(
            message,
            message,
            jax.ShapeDtypeStruct(images.shape, F32),
            jax.ShapeDtypeStruct(nodes.shape, F32),
        ),
        in_specs=[SMEM, HBM, HBM],
        out_specs=(VMEM,) * 4,
        scratch_shapes=[pltpu.SemaphoreType.DMA((5,))],
        compiler_params=pltpu.CompilerParams(vmem_limit_bytes=4 << 20),
        name="pack_rows",
    )(place, in_hbm(images), in_hbm(nodes))


def pack_planes(place, *arrays):
    message = jax.ShapeDtypeStruct((56, 1024), F32)
    return pl.pallas_call(
        pack_planes_kernel,
        out_shape=(message, message),
        in_specs=[SMEM] + [VMEM] * len(arrays),
        out_specs=(VMEM, VMEM),
        compiler_params=pltpu.CompilerParams(vmem_limit_bytes=4 << 20),
        name="pack_planes",
    )(place, *arrays)


def local_part(place, *arrays):
    message = lambda rows: jax.ShapeDtypeStruct((rows, 128), F32)
    constants = build_constants()
    return pl.pallas_call(
        local_kernel,
        out_shape=(
            jax.ShapeDtypeStruct((8, 16, 1024), F32), message(ROWS), message(56), message(48)
        ),
        in_specs=[SMEM] + [VMEM] * 8 + [HBM] * 4,
        out_specs=(VMEM,) * 4,
        scratch_shapes=[
            pltpu.VMEM((4, 16, 1024), F32),
            pltpu.VMEM((3, 2, 32, 1024), F32),
            pltpu.VMEM((8, 1024), F32),
            pltpu.VMEM((24, 1024), F32),
            pltpu.VMEM((288, 1024), F32),
            pltpu.VMEM((288, 1024), F32),
            pltpu.VMEM((24, 128), F32),
            pltpu.VMEM((3, 1, 2, 128), jnp.int32),
            pltpu.VMEM((1024, 384), BF16),
            pltpu.VMEM((256, 1024), BF16),
            pltpu.VMEM((288, 288), BF16),
            pltpu.SemaphoreType.DMA((4,)),
        ],
        compiler_params=pltpu.CompilerParams(vmem_limit_bytes=12 << 20),
        name="local_part",
    )(place, *arrays[:-1], *(in_hbm(a) for a in (arrays[-1],) + constants))


def arrange(place, pieces, data):
    slab, plane = place[0], place[1]
    x_me, y_me = slab // 2, (slab % 2) * 2 + (plane // 2) % 2
    z_me, core = plane // 4, plane % 2

    def step(j, carry):
        bits = [(j >> i) & 1 for i in range(5)]
        for source, half, color, piece in pieces:
            k = core if source == 0 else 1 - core
            first, second = 3 - 2 * k, 1 + 2 * k
            start, count = COLORS[color]
            order = [(color + i) % 3 for i in range(3)]
            delta = [bits[0] * first, bits[1] * first, bits[2] * first]
            delta[order[0]] = delta[order[0]] ^ (bits[3] * second)
            delta[order[1]] = delta[order[1]] ^ (bits[4] * second)
            if half:
                delta[order[2]] = delta[order[2]] ^ second
            x, y, z = x_me ^ delta[0], y_me ^ delta[1], z_me ^ delta[2]
            device = (x * 2 + (y >> 1)) * 16 + z * 4 + (y & 1) * 2 + k
            for t in range(count // 8):
                r = (start + 8 * t) * STRIDE
                data[pl.ds(r + device, 8, stride=STRIDE), :] = piece[j, 8 * t : 8 * t + 8, :]
        return carry

    lax.fori_loop(0, 32, step, 0)


def early_kernel(*refs):
    place, pieces, data = refs[0], refs[1:7], refs[7]
    arrange(place, [(i // 3, 0, i % 3, pieces[i]) for i in range(6)], data)


def middle_kernel(*refs):
    place, pieces, data = refs[0], refs[2:5], refs[5]
    arrange(place, [(0, 1, i, pieces[i]) for i in range(3)], data)


def arranged(kernel, place, pieces, data=None):
    before = () if data is None else (data,)
    return pl.pallas_call(
        kernel,
        out_shape=jax.ShapeDtypeStruct((ROWS * STRIDE, 128), F32),
        in_specs=[SMEM] + [VMEM] * (len(before) + len(pieces)),
        out_specs=VMEM,
        input_output_aliases={} if data is None else {1: 0},
        compiler_params=pltpu.CompilerParams(vmem_limit_bytes=LIMIT_A),
    )(place, *before, *pieces)


def solve_kernel(*refs):
    place, nodes, _ = refs[:3]
    pieces = refs[3:6]
    out, data = refs[6:8]
    var, high, next_row, vec_x, vec_r, vec_p, vec_y = refs[8:]
    slab, plane = place[0], place[1]
    arrange(place, [(1, 1, i, pieces[i]) for i in range(3)], data)

    def field(r):
        return data[r * STRIDE : r * STRIDE + 128, :]

    total = jnp.sum(jnp.sum(field(ENERGY_ROW), axis=0, keepdims=True), axis=1, keepdims=True)
    penalty = reg_weight / (64.0 * 256.0 * 1024.0) * total

    def row_of(tx, tz, yk, ab):
        return ((tx * 2 + tz) * 4 + yk) * 6 + ab

    lane = lax.broadcasted_iota(jnp.int32, (128, 128), 1)
    row = lax.broadcasted_iota(jnp.int32, (128, 128), 0)
    in_plane = row % 16
    first = (lane == 0).astype(F32) + (row < 16).astype(F32)
    first = (first, first)
    first = (first[0] + (in_plane == 0).astype(F32), first[1])
    for ab in (0, 3, 5):
        for yl in range(2):
            for tx, tz, yk, weight in (
                (0, 0, yl, first[yl]), (0, 0, 2 + yl, -1.0), (0, 1, yl, -1.0), (1, 0, yl, -1.0)
            ):
                r = row_of(tx, tz, yk, ab) * STRIDE
                data[r : r + 128, :] = data[r : r + 128, :] + weight * penalty

    def x_next(v):
        return jnp.where(lane < 127, pltpu.roll(v, 127, 1), 0.0)

    def x_prev(v):
        return jnp.where(lane > 0, pltpu.roll(v, 1, 1), 0.0)

    def p_next(v):
        return jnp.where(in_plane < 15, pltpu.roll(v, 127, 0), 0.0)

    def p_prev(v):
        return jnp.where(in_plane > 0, pltpu.roll(v, 1, 0), 0.0)

    zero = jnp.zeros((16, 128), F32)

    def z_next(v):
        return jnp.concatenate([v[16:], zero], axis=0)

    def z_prev(v):
        return jnp.concatenate([zero, v[:112]], axis=0)

    for comp in range(3):
        u = [field(U_ROW + yl * 3 + comp) for yl in range(2)]
        for yl in range(2):
            v = u[yl]
            beside = z_next(v) + z_prev(v) + x_next(v) + x_prev(v)
            beside = beside + (u[1] + p_prev(u[1]) if yl == 0 else u[0] + p_next(u[0]))
            rhs = field(RHS_ROW + yl * 3 + comp) - penalty * (6.0 * v - beside)
            i = comp * 2 + yl
            vec_r[i] = rhs
            vec_p[i] = rhs
            vec_x[i] = jnp.zeros((128, 128), F32)

    def norm():
        value = None
        for i in range(6):
            term = vec_r[i] * vec_r[i]
            value = term if value is None else value + term
        return jnp.sum(jnp.sum(value, axis=0, keepdims=True), axis=1, keepdims=True)

    var[:, 128:144, :] = jnp.zeros((18, 16, 128), F32)
    lane8 = lax.broadcasted_iota(jnp.int32, (8, 128), 1)
    Y_CORNERS = ((0,), (1,), (0, 1), (1, 2))

    def multiply(i, carry):
        here = pl.ds(pl.multiple_of(i * 8, 8), 8)
        above = pl.ds(pl.multiple_of(i * 8 + 16, 8), 8)
        held = (i % 2) * 18
        values = {}
        for z in range(2):
            for b in range(3):
                for y in range(3):
                    for x in range(2):
                        k = (b * 3 + y) * 2 + x
                        values[z, y, x, b] = var[k, above if z else here, :]
        sums = {}

        def add(corner, a, value, sign=1):
            z, y, x = corner
            key = (z, y, x, a)
            if key not in sums:
                sums[key] = high[held + 3 * (y * 2 + x) + a] if z == 0 else None
            old = sums[key]
            if old is None:
                sums[key] = value if sign > 0 else -value
            else:
                sums[key] = old + value if sign > 0 else old - value

        def product(tx, tz, yk, v):
            m = []
            for ab in range(6):
                start = row_of(tx, tz, yk, ab) * STRIDE
                m.append(data[pl.ds(pl.multiple_of(start + i * 8, 8), 8), :])
            return [m[AB[a][0]] * v[0] + m[AB[a][1]] * v[1] + m[AB[a][2]] * v[2] for a in range(3)]

        for tz in range(2):
            for tx in range(2):
                for yk in range(4):
                    ys = Y_CORNERS[yk]
                    if tz == 0 and tx == 0 and yk < 2:
                        v = [values[0, ys[0], 0, b] for b in range(3)]
                        for a, q in enumerate(product(tx, tz, yk, v)):
                            add((0, ys[0], 0), a, q)
                        continue
                    ends = []
                    for oz in range(1 + tz):
                        for oy in range(len(ys)):
                            for ox in range(1 + tx):
                                one = (oz, ys[oy], ox)
                                two = (tz - oz, ys[len(ys) - 1 - oy], tx - ox)
                                if (two, one) not in ends:
                                    ends.append((one, two))
                    for one, two in ends:
                        v = [values[two + (b,)] - values[one + (b,)] for b in range(3)]
                        for a, q in enumerate(product(tx, tz, yk, v)):
                            add(one, a, q)
                            add(two, a, q, -1)
        for a in range(3):
            for y in range(3):
                part = sums[0, y, 0, a] + jnp.where(
                    lane8 > 0, pltpu.roll(sums[0, y, 1, a], 1, 1), 0.0
                )
                if y < 2:
                    vec_y[a * 2 + y, here, :] = part
                else:
                    next_row[a, here, :] = part
                for x in range(2):
                    high[held + 3 * (y * 2 + x) + a] = sums[1, y, x, a]
        return carry

    def apply():
        for comp in range(3):
            own = [vec_p[comp * 2 + yl] for yl in range(2)]
            for y_kind, v in enumerate((own[0], own[1], p_next(own[0]))):
                i = (comp * 3 + y_kind) * 2
                var[i, 0:128, :] = v
                var[i + 1, 0:128, :] = x_next(v)
        high[...] = jnp.zeros((36, 8, 128), F32)
        lax.fori_loop(0, 16, multiply, 0)
        energy = None
        for comp in range(3):
            vec_y[comp * 2] = vec_y[comp * 2] + p_prev(next_row[comp])
            for yl in range(2):
                term = vec_y[comp * 2 + yl] * vec_p[comp * 2 + yl]
                energy = term if energy is None else energy + term
        curvature = jnp.sum(jnp.sum(energy, axis=0, keepdims=True), axis=1, keepdims=True)
        return curvature

    def sweep(step, norm_now):
        size = norm_now / apply()
        for i in range(6):
            vec_x[i] = vec_x[i] + size * vec_p[i]
            vec_r[i] = vec_r[i] - size * vec_y[i]
        norm_next = norm()
        ratio = norm_next / norm_now
        for i in range(6):
            vec_p[i] = vec_r[i] + ratio * vec_p[i]
        return norm_next

    norm_last = lax.fori_loop(0, ITERS - 1, sweep, norm())
    size = norm_last / apply()
    mine = slab * 16 + plane
    for comp in range(3):
        for yl in range(2):
            out[comp, 0, yl : yl + 1, :] = (
                nodes[comp, 0, yl : yl + 1, :]
                + vec_x[comp * 2 + yl, pl.ds(mine, 1), :]
                + size * vec_p[comp * 2 + yl, pl.ds(mine, 1), :]
            )


def solve_part(place, nodes, data, pieces):
    return pl.pallas_call(
        solve_kernel,
        out_shape=(
            jax.ShapeDtypeStruct((3, 1, 2, 128), F32),
            jax.ShapeDtypeStruct((ROWS * STRIDE, 128), F32),
        ),
        in_specs=[SMEM] + [VMEM] * 5,
        out_specs=(VMEM, VMEM),
        input_output_aliases={2: 1},
        scratch_shapes=[
            pltpu.VMEM((18, 144, 128), F32),
            pltpu.VMEM((36, 8, 128), F32),
            pltpu.VMEM((3, 128, 128), F32),
        ]
        + [pltpu.VMEM((6, 128, 128), F32)] * 4,
        compiler_params=pltpu.CompilerParams(vmem_limit_bytes=LIMIT_B),
        name="solve_part",
    )(place, nodes, data, *pieces)[0]


def coordinates(device):
    slab, plane = divmod(device, 16)
    x, y_hi = divmod(slab, 2)
    z, rest = divmod(plane, 4)
    y_lo, core = divmod(rest, 2)
    return [x, y_hi * 2 + y_lo, z, core]


def device_of(x, y, z, core):
    return (x * 2 + y // 2) * 16 + z * 4 + (y % 2) * 2 + core


def exchange(value, axis, second):
    pairs = []
    for device in range(128):
        at = coordinates(device)
        if axis == 3:
            at[3] = 1 - at[3]
        else:
            at[axis] ^= 3 if (at[3] == 1) == second else 1
        pairs.append((device, device_of(*at)))
    return lax.ppermute(value, AXES, pairs)


def shifted(value, slab_step, plane_step):
    pairs = []
    for slab in range(8 - slab_step):
        for plane in range(16 - plane_step):
            pairs.append((slab * 16 + plane, (slab + slab_step) * 16 + plane + plane_step))
    return lax.ppermute(value, AXES, pairs)


def swap(value, axis, second):
    count = lax.axis_size(axis)
    pairs = []
    for i in range(count):
        j = i + (1 if (i % 2 == 1) == second else -1)
        if 0 <= j < count:
            pairs.append((i, j))
    return lax.ppermute(value, axis, pairs)


def program(images, shifts, nodes):
    place = jnp.stack([lax.axis_index("slab"), lax.axis_index("plane")]).astype(jnp.int32)
    first, second, images, nodes = pack_rows(place, images, nodes)
    rows = swap(first, "plane", False), swap(second, "plane", True)
    first, second = pack_planes(place, images, nodes, *rows)
    planes = swap(first, "slab", False), swap(second, "slab", True)
    inner = inner_part(place, images, *rows)
    mismatch, own, to_slab, to_plane = local_part(place, *inner, *planes, *rows, nodes, shifts)

    def spaced(value, layout):
        rows = []
        for start, count, gap in layout:
            rows += [value[start : start + count], jnp.zeros((gap, 128), F32)]
        return jnp.concatenate(rows, 0)

    got = shifted(to_plane, 0, 1)
    to_slab = to_slab + spaced(got, ((24, 6, 18), (30, 6, 18), (39, 3, 5)))
    own = own + spaced(got, ((0, 6, 18), (6, 6, 18), (12, 6, 18), (18, 6, 18), (36, 3, 13)))
    got = shifted(to_slab, 1, 0)
    payload = own + spaced(got, ((0, 24, 24), (24, 24, 24), (48, 6, 10)))
    blocks = payload[None]
    for axis in range(3):
        blocks = jnp.concatenate([blocks, exchange(blocks, axis, False)], 0)
    parts = [blocks[:, start : start + count] for start, count in COLORS]
    for turn in range(2):
        parts = [
            jnp.concatenate([part, exchange(part, (color + turn) % 3, True)], 0)
            for color, part in enumerate(parts)
        ]
    last = []
    for color, part in enumerate(parts):
        last.append(exchange(part, (color + 2) % 3, True))
    other = []
    for part in parts:
        other.append(exchange(part, 3, False))
    data = arranged(early_kernel, place, parts + other)
    data = arranged(middle_kernel, place, last, data)
    other = []
    for part in last:
        other.append(exchange(part, 3, False))
    result = solve_part(place, nodes, data, other)
    return result, mismatch


def solution(mesh):
    in_specs = (
        P(None, "slab", "plane", None),
        P(None, "slab", "plane", None),
        P(None, "slab", "plane", None),
    )
    out_specs = (P(None, "slab", "plane", None), P("slab", "plane", None))
    return jax.shard_map(program, mesh=mesh, in_specs=in_specs, out_specs=out_specs, check_vma=False)
```

```python
import jax
import jax.numpy as jnp
import numpy as np
from jax import lax
from jax.experimental import pallas as pl
from jax.experimental.pallas import tpu as pltpu
from jax.sharding import PartitionSpec as P


ITERS = 6
reg_weight = 4.0
AXES = ("slab", "plane")
NCHUNK = 8
ROWS = 112
RHS_ROW = 96
U_ROW = 102
ENERGY_ROW = 108
COLORS = ((0, 40), (40, 40), (80, 32))
STRIDE = 136
LIMIT_A = 2 << 20
LIMIT_B = 9 << 20
PAIRS = ((0, 0), (0, 1), (0, 2), (1, 1), (1, 2), (2, 2))
AB = [[0, 1, 2], [1, 3, 4], [2, 4, 5]]
F32 = jnp.float32
BF16 = jnp.bfloat16


def build_constants():
    w = np.arange(8) / 8.0
    lo, up = 1.0 - w, w
    quad = (lo * lo, lo * up, up * up)
    lin = (lo, up)
    wq = np.zeros((1024, 256))
    wl = np.zeros((1024, 128))
    for e in range(128):
        for i in range(8):
            v = 8 * e + i
            wq[v, e] += quad[0][i]
            wq[v, 128 + e] += quad[1][i]
            wl[v, e] += lin[0][i]
            if e + 1 < 128:
                wq[v, e + 1] += quad[2][i]
                wl[v, e + 1] += lin[1][i]
    spread = np.zeros((128, 1024))
    for e in range(128):
        spread[e, 8 * e : 8 * e + 8] = 1.0
    ly = np.zeros((4, 48, 288))
    ry = np.zeros((4, 24, 288))

    def put(which, tz, yk, zt, er, yq):
        for ab in range(6):
            for s in range(8):
                ly[which, (tz * 4 + yk) * 6 + ab, ((zt * 6 + ab) * 2 + er) * 8 + s] += quad[yq][s]

    for which, tz, zt in ((0, 0, 0), (0, 1, 1), (1, 0, 2)):
        put(which, tz, 0, zt, 0, 0)
        put(which, tz, 1, zt, 0, 2)
        put(which, tz, 1, zt, 1, 0)
        put(which, tz, 2, zt, 0, 1)
        put(which, tz, 3, zt, 1, 1)
    for which, tz, zt in ((2, 0, 0), (2, 1, 1), (3, 0, 2)):
        put(which, tz, 0, zt, 1, 2)

    def put_rhs(which, yl, zt, er, yq):
        for c in range(9):
            for s in range(8):
                ry[which, yl * 9 + c, ((zt * 9 + c) * 2 + er) * 8 + s] += lin[yq][s]

    for which, zt in ((0, 0), (1, 1)):
        put_rhs(which, 0, zt, 0, 0)
        put_rhs(which, 1, zt, 0, 1)
        put_rhs(which, 1, zt, 1, 0)
    for which, zt in ((2, 0), (3, 1)):
        put_rhs(which, 0, zt, 1, 1)
    cast = lambda a: jnp.asarray(a.astype(np.float32)).astype(BF16)
    return (
        cast(np.concatenate([wq, wl], 1)),
        cast(np.concatenate([wl.T, spread], 0)),
        cast(np.concatenate([ly.reshape(192, 288), ry.reshape(96, 288)], 0)),
    )


def dot(a, b):
    return lax.dot_general(a, b, (((1,), (0,)), ((), ())), preferred_element_type=F32)


def split_left(a, b, parts=2):
    total = None
    for _ in range(parts):
        piece = a.astype(BF16)
        a = a - piece.astype(F32)
        term = dot(piece, b)
        total = term if total is None else total + term
    return total


def split_right(a, b, parts=2):
    total = None
    for _ in range(parts):
        piece = b.astype(BF16)
        b = b - piece.astype(F32)
        term = dot(a, piece)
        total = term if total is None else total + term
    return total


def by_parity(odd, run, one, two):
    @pl.when(odd == 0)
    def _():
        run(one, two)

    @pl.when(odd == 1)
    def _():
        run(two, one)


def pack_rows_kernel(place, images_in, nodes_in, first_send, second_send, images, nodes, sems):
    copies = [pltpu.make_async_copy(nodes_in, nodes, sems.at[4])]
    for i in range(2):
        for k in range(2):
            part = (i, pl.ds(4 * k, 4))
            copies.append(
                pltpu.make_async_copy(images_in.at[part], images.at[part], sems.at[2 * i + k])
            )
    for copy in copies:
        copy.start()
    for copy in copies:
        copy.wait()

    def fill(last, first):
        for z in range(8):
            last[2 * z : 2 * z + 2, :] = images[0, z, 14:16, :]
            last[16 + z : 17 + z, :] = images[1, z, 15:16, :]
            first[2 * z : 2 * z + 2, :] = images[0, z, 0:2, :]
            first[16 + z : 17 + z, :] = images[1, z, 0:1, :]
        last[24:32, :] = jnp.zeros((8, 1024), F32)
        first[24:32, :] = jnp.zeros((8, 1024), F32)
        for c in range(3):
            first[24:25, 128 * c : 128 * c + 128] = nodes[c, 0, 0:1, :]

    by_parity(place[1] % 2, fill, first_send, second_send)


def pack_planes_kernel(place, images, nodes, first_rows, second_rows, first_send, second_send):
    def fill(forward, backward):
        for target, planes in ((forward, (6, 7, 7)), (backward, (0, 1, 0))):
            target[0:16, :] = images[0, planes[0]]
            target[16:32, :] = images[0, planes[1]]
            target[32:48, :] = images[1, planes[2]]
        forward[48:56, :] = jnp.zeros((8, 1024), F32)
        backward[48:56, :] = jnp.zeros((8, 1024), F32)

        def corners(high, low):
            for target, z in ((forward, 7), (backward, 0)):
                target[48:49, :] = low[16 + z : 17 + z, :]
                target[49:50, :] = high[16 + z : 17 + z, :]
            for c in range(3):
                for y in range(3):
                    i = c * 3 + y
                    source = nodes[c, 0, y : y + 1, :] if y < 2 else high[24:25, 128 * c : 128 * c + 128]
                    at = 128 * (i % 8)
                    backward[50 + i // 8 : 51 + i // 8, at : at + 128] = source

        by_parity(place[1] % 2, corners, first_rows, second_rows)

    by_parity(place[0] % 2, fill, first_send, second_send)


def shift_lanes(value, off):
    lane = lax.broadcasted_iota(jnp.int32, (1, 1024), 1)
    moved = pltpu.roll(value, (-off) % 1024, value.ndim - 1)
    inside = (lane + off >= 0) & (lane + off < 1024)
    return jnp.where(inside, moved, 0.0)


def inner_kernel(place, images, first_rows, second_rows, mid0, mid1, gx):
    mid0[:, 8:24, :] = images[0]
    mid1[1, :, 8:24, :] = images[1]

    def put_rows(high, low):
        for z in range(8):
            mid0[z, 6:8, :] = low[2 * z : 2 * z + 2, :]
            mid0[z, 24:26, :] = high[2 * z : 2 * z + 2, :]
            mid1[1, z, 7:8, :] = low[16 + z : 17 + z, :]
            mid1[1, z, 24:25, :] = high[16 + z : 17 + z, :]

    by_parity(place[1] % 2, put_rows, first_rows, second_rows)

    def along_x(z, carry):
        plane = mid1[1, z]
        mid1[0, z] = shift_lanes(plane, -1)
        mid1[2, z] = shift_lanes(plane, 1)
        t = images[0, z]
        near = shift_lanes(t, 1) - shift_lanes(t, -1)
        gx[z] = (shift_lanes(t, -2) - shift_lanes(t, 2) + 8.0 * near) * (1.0 / 12.0)
        return carry

    lax.fori_loop(0, 8, along_x, 0)


def inner_part(place, images, *rows):
    return pl.pallas_call(
        inner_kernel,
        out_shape=(
            jax.ShapeDtypeStruct((8, 32, 1024), F32),
            jax.ShapeDtypeStruct((3, 8, 32, 1024), F32),
            jax.ShapeDtypeStruct((8, 16, 1024), F32),
        ),
        in_specs=[SMEM] + [VMEM] * 3,
        out_specs=(VMEM,) * 3,
        compiler_params=pltpu.CompilerParams(vmem_limit_bytes=8 << 20),
        name="inner_part",
    )(place, images, *rows)


def local_kernel(
    place, mid0, mid1, gx, first_planes, second_planes, first_rows, second_rows, nodes,
    shifts_in, to_nodes_in, to_voxels_in, down_rows_in,
    mismatch, own, to_slab, to_plane,
    out0, out1, sh, un, acc, acc_rhs, near, shifts, to_nodes, to_voxels, down_rows, sems,
):
    pairs = (
        (shifts_in, shifts), (to_voxels_in, to_voxels), (to_nodes_in, to_nodes),
        (down_rows_in, down_rows),
    )
    copies = [pltpu.make_async_copy(a, b, sems.at[i]) for i, (a, b) in enumerate(pairs)]
    for copy in copies:
        copy.start()
    near[...] = jnp.zeros((24, 128), F32)
    for c in range(3):
        near[6 * c : 6 * c + 2, :] = nodes[c, 0]

    def put_planes(high, low):
        out0[0:2] = low[0:32, :].reshape(2, 16, 1024)
        out0[2:4] = high[0:32, :].reshape(2, 16, 1024)
        for k, source in ((0, low), (1, high)):
            out1[1, k, 8:24, :] = source[32:48, :]
            out1[1, k, 7:8, :] = source[48:49, :]
            out1[1, k, 24:25, :] = source[49:50, :]
        for c in range(3):
            for y in range(3):
                i = c * 3 + y
                at = 128 * (i % 8)
                r = 6 * c + 3 + y
                near[r : r + 1, :] = high[50 + i // 8 : 51 + i // 8, at : at + 128]

    def put_rows(high, low):
        for c in range(3):
            near[6 * c + 2 : 6 * c + 3, :] = high[24:25, 128 * c : 128 * c + 128]

    by_parity(place[0] % 2, put_planes, first_planes, second_planes)
    by_parity(place[1] % 2, put_rows, first_rows, second_rows)
    for k in range(2):
        plane = out1[1, k]
        out1[0, k] = shift_lanes(plane, -1)
        out1[2, k] = shift_lanes(plane, 1)
    copies[0].wait()
    copies[1].wait()
    for c in range(3):
        sh[2 * c : 2 * c + 2, :] = dot(shifts[c, 0].astype(F32).astype(BF16), to_voxels[128:256, :])
    un[...] = split_left(near[...], to_voxels[0:128, :], 3)
    wy = lax.broadcasted_iota(jnp.int32, (8, 128), 0).astype(F32) * 0.125

    def chunk(c, energy):
        at = pl.ds(pl.multiple_of(c * 128, 128), 128)
        for er in range(2):
            base = 8 + 8 * er

            def full(row):
                return jnp.broadcast_to(row, (8, 128))

            sz = full(sh[er : er + 1, at])
            sy = full(sh[2 + er : 3 + er, at])
            sx = full(sh[4 + er : 5 + er, at])
            x_low, x_up = sx < -0.5, sx > 0.5
            y_low, y_up = sy < -0.5, sy > 0.5
            z_low, z_up = sz < -0.5, sz > 0.5

            def in_plane(k):
                rows = []
                for dy in (-1, 0, 1):
                    ref, i = (mid1, k - 1) if 1 <= k <= 8 else (out1, k // 9)
                    a, b, d = (ref[n, i, base + dy : base + dy + 8, at] for n in range(3))
                    rows.append(jnp.where(x_low, a, jnp.where(x_up, d, b)))
                return jnp.where(y_low, rows[0], jnp.where(y_up, rows[2], rows[1]))

            corner = []
            for comp in range(3):
                for zn in range(2):
                    i = (comp * 2 + zn) * 3 + er
                    first, second = full(un[i : i + 1, at]), full(un[i + 1 : i + 2, at])
                    corner.append(first + wy * (second - first))
            sums = [None] * 18
            sums_rhs = [None] * 6
            planes = [in_plane(0), in_plane(1)]
            for z in range(8):
                planes.append(in_plane(z + 2))
                warped = jnp.where(z_low, planes[z], jnp.where(z_up, planes[z + 2], planes[z + 1]))

                def here(k):
                    if 2 <= k <= 9:
                        return mid0[k - 2, base : base + 8, at]
                    return out0[k if k < 2 else k - 8, base - 8 : base, at]

                rows = lambda dy: mid0[z, base + dy : base + dy + 8, at]
                g0 = (here(z) - here(z + 4) + 8.0 * (here(z + 3) - here(z + 1))) * (1.0 / 12.0)
                g1 = (rows(-2) - rows(2) + 8.0 * (rows(1) - rows(-1))) * (1.0 / 12.0)
                g2 = gx[z, base - 8 : base, at]
                g = (g0, g1, g2)
                w = z / 8.0
                total = None
                for comp in range(3):
                    moved = corner[2 * comp] + w * (corner[2 * comp + 1] - corner[2 * comp])
                    term = g[comp] * moved
                    total = term if total is None else total + term
                mis = here(z + 2) - warped - total
                mismatch[z, base - 8 : base, at] = mis

                def add(store, i, weight, value):
                    if weight:
                        term = value if weight == 1.0 else weight * value
                        store[i] = term if store[i] is None else store[i] + term

                for ab, (a, b) in enumerate(PAIRS):
                    prod = g[a] * g[b]
                    if a == b:
                        energy = energy + prod
                    for zt, weight in enumerate(((1 - w) * (1 - w), w * (1 - w), w * w)):
                        add(sums, zt * 6 + ab, weight, prod)
                for comp in range(3):
                    prod = g[comp] * mis
                    for zt, weight in enumerate((1 - w, w)):
                        add(sums_rhs, zt * 3 + comp, weight, prod)
            for i in range(18):
                r = (i * 2 + er) * 8
                acc[r : r + 8, at] = sums[i]
            for zt in range(2):
                for c in range(9):
                    r = ((zt * 9 + c) * 2 + er) * 8
                    if c < 3:
                        value = sums_rhs[zt * 3 + c]
                    else:
                        value = sums[zt * 6 + c - 3] + sums[zt * 6 + c + 3]
                    acc_rhs[r : r + 8, at] = value
        return energy

    energy = lax.fori_loop(0, NCHUNK, chunk, jnp.zeros((8, 128), F32))
    copies[2].wait()
    copies[3].wait()
    by_x = split_left(acc[...], to_nodes[:, 0:256])
    by_x_rhs = split_left(acc_rhs[...], to_nodes[:, 256:384])
    by_y = split_right(down_rows[0:192, :], by_x)
    by_y_rhs = split_right(down_rows[192:288, :], by_x_rhs)

    def edges(which, tx, first, count):
        r = 48 * which + first
        return by_y[r : r + count, 128 * tx : 128 * tx + 128]

    def whole(which, yl):
        r = 24 * which + 9 * yl
        return by_y_rhs[r + 3 : r + 9, :]

    def load(which, yl):
        r = 24 * which + 9 * yl
        return by_y_rhs[r : r + 3, :]

    own[0:6, :] = whole(0, 0)
    own[6:12, :] = whole(0, 1)
    own[12:48, :] = edges(0, 0, 12, 36)
    own[48:96, :] = edges(0, 1, 0, 48)
    own[96:99, :] = load(0, 0)
    own[99:102, :] = load(0, 1)
    own[108:112, :] = jnp.zeros((4, 128), F32)
    to_slab[0:6, :] = whole(1, 0)
    to_slab[6:12, :] = whole(1, 1)
    to_slab[12:24, :] = edges(1, 0, 12, 12)
    to_slab[24:48, :] = edges(1, 1, 0, 24)
    to_slab[48:51, :] = load(1, 0)
    to_slab[51:54, :] = load(1, 1)
    to_slab[54:56, :] = jnp.zeros((2, 128), F32)
    to_plane[0:6, :] = whole(2, 0)
    to_plane[6:12, :] = edges(2, 0, 24, 6)
    to_plane[12:18, :] = edges(2, 1, 0, 6)
    to_plane[18:24, :] = edges(2, 1, 24, 6)
    to_plane[24:30, :] = whole(3, 0)
    to_plane[30:36, :] = edges(3, 1, 0, 6)
    to_plane[36:39, :] = load(2, 0)
    to_plane[39:42, :] = load(3, 0)
    to_plane[42:48, :] = jnp.zeros((6, 128), F32)
    for yl in range(2):
        for comp in range(3):
            r = U_ROW + yl * 3 + comp
            own[r : r + 1, :] = nodes[comp, 0, yl : yl + 1, :]
    own[ENERGY_ROW : ENERGY_ROW + 1, :] = jnp.sum(energy, axis=0, keepdims=True)


VMEM = pl.BlockSpec(memory_space=pltpu.VMEM)
SMEM = pl.BlockSpec(memory_space=pltpu.SMEM)
HBM = pl.BlockSpec(memory_space=pltpu.HBM)


def in_hbm(array):
    return pltpu.with_memory_space_constraint(array, pltpu.HBM)


def pack_rows(place, images, nodes):
    message = jax.ShapeDtypeStruct((32, 1024), F32)
    return pl.pallas_call(
        pack_rows_kernel,
        out_shape=(
            message,
            message,
            jax.ShapeDtypeStruct(images.shape, F32),
            jax.ShapeDtypeStruct(nodes.shape, F32),
        ),
        in_specs=[SMEM, HBM, HBM],
        out_specs=(VMEM,) * 4,
        scratch_shapes=[pltpu.SemaphoreType.DMA((5,))],
        compiler_params=pltpu.CompilerParams(vmem_limit_bytes=4 << 20),
        name="pack_rows",
    )(place, in_hbm(images), in_hbm(nodes))


def pack_planes(place, *arrays):
    message = jax.ShapeDtypeStruct((56, 1024), F32)
    return pl.pallas_call(
        pack_planes_kernel,
        out_shape=(message, message),
        in_specs=[SMEM] + [VMEM] * len(arrays),
        out_specs=(VMEM, VMEM),
        compiler_params=pltpu.CompilerParams(vmem_limit_bytes=4 << 20),
        name="pack_planes",
    )(place, *arrays)


def local_part(place, *arrays):
    message = lambda rows: jax.ShapeDtypeStruct((rows, 128), F32)
    constants = build_constants()
    return pl.pallas_call(
        local_kernel,
        out_shape=(
            jax.ShapeDtypeStruct((8, 16, 1024), F32), message(ROWS), message(56), message(48)
        ),
        in_specs=[SMEM] + [VMEM] * 8 + [HBM] * 4,
        out_specs=(VMEM,) * 4,
        scratch_shapes=[
            pltpu.VMEM((4, 16, 1024), F32),
            pltpu.VMEM((3, 2, 32, 1024), F32),
            pltpu.VMEM((8, 1024), F32),
            pltpu.VMEM((24, 1024), F32),
            pltpu.VMEM((288, 1024), F32),
            pltpu.VMEM((288, 1024), F32),
            pltpu.VMEM((24, 128), F32),
            pltpu.VMEM((3, 1, 2, 128), jnp.int32),
            pltpu.VMEM((1024, 384), BF16),
            pltpu.VMEM((256, 1024), BF16),
            pltpu.VMEM((288, 288), BF16),
            pltpu.SemaphoreType.DMA((4,)),
        ],
        compiler_params=pltpu.CompilerParams(vmem_limit_bytes=12 << 20),
        name="local_part",
    )(place, *arrays[:-1], *(in_hbm(a) for a in (arrays[-1],) + constants))


def arrange(place, pieces, data):
    slab, plane = place[0], place[1]
    x_me, y_me = slab // 2, (slab % 2) * 2 + (plane // 2) % 2
    z_me, core = plane // 4, plane % 2

    def step(j, carry):
        bits = [(j >> i) & 1 for i in range(5)]
        for source, half, color, piece in pieces:
            k = core if source == 0 else 1 - core
            first, second = 3 - 2 * k, 1 + 2 * k
            start, count = COLORS[color]
            order = [(color + i) % 3 for i in range(3)]
            delta = [bits[0] * first, bits[1] * first, bits[2] * first]
            delta[order[0]] = delta[order[0]] ^ (bits[3] * second)
            delta[order[1]] = delta[order[1]] ^ (bits[4] * second)
            if half:
                delta[order[2]] = delta[order[2]] ^ second
            x, y, z = x_me ^ delta[0], y_me ^ delta[1], z_me ^ delta[2]
            device = (x * 2 + (y >> 1)) * 16 + z * 4 + (y & 1) * 2 + k
            for t in range(count // 8):
                r = (start + 8 * t) * STRIDE
                data[pl.ds(r + device, 8, stride=STRIDE), :] = piece[j, 8 * t : 8 * t + 8, :]
        return carry

    lax.fori_loop(0, 32, step, 0)


def early_kernel(*refs):
    place, pieces, data = refs[0], refs[1:7], refs[7]
    arrange(place, [(i // 3, 0, i % 3, pieces[i]) for i in range(6)], data)


def middle_kernel(*refs):
    place, pieces, data = refs[0], refs[2:5], refs[5]
    arrange(place, [(0, 1, i, pieces[i]) for i in range(3)], data)


def arranged(kernel, place, pieces, data=None):
    before = () if data is None else (data,)
    return pl.pallas_call(
        kernel,
        out_shape=jax.ShapeDtypeStruct((ROWS * STRIDE, 128), F32),
        in_specs=[SMEM] + [VMEM] * (len(before) + len(pieces)),
        out_specs=VMEM,
        input_output_aliases={} if data is None else {1: 0},
        compiler_params=pltpu.CompilerParams(vmem_limit_bytes=LIMIT_A),
    )(place, *before, *pieces)


def solve_kernel(*refs):
    place, nodes, _ = refs[:3]
    pieces = refs[3:6]
    out, data = refs[6:8]
    var, high, next_row, vec_x, vec_r, vec_p, vec_y = refs[8:]
    slab, plane = place[0], place[1]
    arrange(place, [(1, 1, i, pieces[i]) for i in range(3)], data)

    def field(r):
        return data[r * STRIDE : r * STRIDE + 128, :]

    total = jnp.sum(jnp.sum(field(ENERGY_ROW), axis=0, keepdims=True), axis=1, keepdims=True)
    penalty = reg_weight / (64.0 * 256.0 * 1024.0) * total

    def row_of(tx, tz, yk, ab):
        return ((tx * 2 + tz) * 4 + yk) * 6 + ab

    lane = lax.broadcasted_iota(jnp.int32, (128, 128), 1)
    row = lax.broadcasted_iota(jnp.int32, (128, 128), 0)
    in_plane = row % 16
    first = (lane == 0).astype(F32) + (row < 16).astype(F32)
    first = (first, first)
    first = (first[0] + (in_plane == 0).astype(F32), first[1])
    for ab in (0, 3, 5):
        for yl in range(2):
            for tx, tz, yk, weight in (
                (0, 0, yl, first[yl]), (0, 0, 2 + yl, -1.0), (0, 1, yl, -1.0), (1, 0, yl, -1.0)
            ):
                r = row_of(tx, tz, yk, ab) * STRIDE
                data[r : r + 128, :] = data[r : r + 128, :] + weight * penalty

    def x_next(v):
        return jnp.where(lane < 127, pltpu.roll(v, 127, 1), 0.0)

    def x_prev(v):
        return jnp.where(lane > 0, pltpu.roll(v, 1, 1), 0.0)

    def p_next(v):
        return jnp.where(in_plane < 15, pltpu.roll(v, 127, 0), 0.0)

    def p_prev(v):
        return jnp.where(in_plane > 0, pltpu.roll(v, 1, 0), 0.0)

    zero = jnp.zeros((16, 128), F32)

    def z_next(v):
        return jnp.concatenate([v[16:], zero], axis=0)

    def z_prev(v):
        return jnp.concatenate([zero, v[:112]], axis=0)

    for comp in range(3):
        u = [field(U_ROW + yl * 3 + comp) for yl in range(2)]
        for yl in range(2):
            v = u[yl]
            beside = z_next(v) + z_prev(v) + x_next(v) + x_prev(v)
            beside = beside + (u[1] + p_prev(u[1]) if yl == 0 else u[0] + p_next(u[0]))
            rhs = field(RHS_ROW + yl * 3 + comp) - penalty * (6.0 * v - beside)
            i = comp * 2 + yl
            vec_r[i] = rhs
            vec_p[i] = rhs
            vec_x[i] = jnp.zeros((128, 128), F32)

    def norm():
        value = None
        for i in range(6):
            term = vec_r[i] * vec_r[i]
            value = term if value is None else value + term
        return jnp.sum(jnp.sum(value, axis=0, keepdims=True), axis=1, keepdims=True)

    var[:, 128:144, :] = jnp.zeros((18, 16, 128), F32)
    lane8 = lax.broadcasted_iota(jnp.int32, (8, 128), 1)
    Y_CORNERS = ((0,), (1,), (0, 1), (1, 2))

    def multiply(i, carry):
        here = pl.ds(pl.multiple_of(i * 8, 8), 8)
        above = pl.ds(pl.multiple_of(i * 8 + 16, 8), 8)
        held = (i % 2) * 18
        values = {}
        for z in range(2):
            for b in range(3):
                for y in range(3):
                    for x in range(2):
                        k = (b * 3 + y) * 2 + x
                        values[z, y, x, b] = var[k, above if z else here, :]
        sums = {}

        def add(corner, a, value, sign=1):
            z, y, x = corner
            key = (z, y, x, a)
            if key not in sums:
                sums[key] = high[held + 3 * (y * 2 + x) + a] if z == 0 else None
            old = sums[key]
            if old is None:
                sums[key] = value if sign > 0 else -value
            else:
                sums[key] = old + value if sign > 0 else old - value

        def product(tx, tz, yk, v):
            m = []
            for ab in range(6):
                start = row_of(tx, tz, yk, ab) * STRIDE
                m.append(data[pl.ds(pl.multiple_of(start + i * 8, 8), 8), :])
            return [m[AB[a][0]] * v[0] + m[AB[a][1]] * v[1] + m[AB[a][2]] * v[2] for a in range(3)]

        for tz in range(2):
            for tx in range(2):
                for yk in range(4):
                    ys = Y_CORNERS[yk]
                    if tz == 0 and tx == 0 and yk < 2:
                        v = [values[0, ys[0], 0, b] for b in range(3)]
                        for a, q in enumerate(product(tx, tz, yk, v)):
                            add((0, ys[0], 0), a, q)
                        continue
                    ends = []
                    for oz in range(1 + tz):
                        for oy in range(len(ys)):
                            for ox in range(1 + tx):
                                one = (oz, ys[oy], ox)
                                two = (tz - oz, ys[len(ys) - 1 - oy], tx - ox)
                                if (two, one) not in ends:
                                    ends.append((one, two))
                    for one, two in ends:
                        v = [values[two + (b,)] - values[one + (b,)] for b in range(3)]
                        for a, q in enumerate(product(tx, tz, yk, v)):
                            add(one, a, q)
                            add(two, a, q, -1)
        for a in range(3):
            for y in range(3):
                part = sums[0, y, 0, a] + jnp.where(
                    lane8 > 0, pltpu.roll(sums[0, y, 1, a], 1, 1), 0.0
                )
                if y < 2:
                    vec_y[a * 2 + y, here, :] = part
                else:
                    next_row[a, here, :] = part
                for x in range(2):
                    high[held + 3 * (y * 2 + x) + a] = sums[1, y, x, a]
        return carry

    def sweep(step, norm_now):
        for comp in range(3):
            own = [vec_p[comp * 2 + yl] for yl in range(2)]
            for y_kind, v in enumerate((own[0], own[1], p_next(own[0]))):
                i = (comp * 3 + y_kind) * 2
                var[i, 0:128, :] = v
                var[i + 1, 0:128, :] = x_next(v)
        high[...] = jnp.zeros((36, 8, 128), F32)
        lax.fori_loop(0, 16, multiply, 0, unroll=2)
        energy = None
        for comp in range(3):
            vec_y[comp * 2] = vec_y[comp * 2] + p_prev(next_row[comp])
            for yl in range(2):
                term = vec_y[comp * 2 + yl] * vec_p[comp * 2 + yl]
                energy = term if energy is None else energy + term
        curvature = jnp.sum(jnp.sum(energy, axis=0, keepdims=True), axis=1, keepdims=True)
        size = norm_now / curvature
        for i in range(6):
            vec_x[i] = vec_x[i] + size * vec_p[i]
            vec_r[i] = vec_r[i] - size * vec_y[i]
        norm_next = norm()
        ratio = norm_next / norm_now
        for i in range(6):
            vec_p[i] = vec_r[i] + ratio * vec_p[i]
        return norm_next

    lax.fori_loop(0, ITERS, sweep, norm())
    mine = slab * 16 + plane
    for comp in range(3):
        for yl in range(2):
            out[comp, 0, yl : yl + 1, :] = (
                nodes[comp, 0, yl : yl + 1, :] + vec_x[comp * 2 + yl, pl.ds(mine, 1), :]
            )


def solve_part(place, nodes, data, pieces):
    return pl.pallas_call(
        solve_kernel,
        out_shape=(
            jax.ShapeDtypeStruct((3, 1, 2, 128), F32),
            jax.ShapeDtypeStruct((ROWS * STRIDE, 128), F32),
        ),
        in_specs=[SMEM] + [VMEM] * 5,
        out_specs=(VMEM, VMEM),
        input_output_aliases={2: 1},
        scratch_shapes=[
            pltpu.VMEM((18, 144, 128), F32),
            pltpu.VMEM((36, 8, 128), F32),
            pltpu.VMEM((3, 128, 128), F32),
        ]
        + [pltpu.VMEM((6, 128, 128), F32)] * 4,
        compiler_params=pltpu.CompilerParams(vmem_limit_bytes=LIMIT_B),
        name="solve_part",
    )(place, nodes, data, *pieces)[0]


def coordinates(device):
    slab, plane = divmod(device, 16)
    x, y_hi = divmod(slab, 2)
    z, rest = divmod(plane, 4)
    y_lo, core = divmod(rest, 2)
    return [x, y_hi * 2 + y_lo, z, core]


def device_of(x, y, z, core):
    return (x * 2 + y // 2) * 16 + z * 4 + (y % 2) * 2 + core


def exchange(value, axis, second):
    pairs = []
    for device in range(128):
        at = coordinates(device)
        if axis == 3:
            at[3] = 1 - at[3]
        else:
            at[axis] ^= 3 if (at[3] == 1) == second else 1
        pairs.append((device, device_of(*at)))
    return lax.ppermute(value, AXES, pairs)


def shifted(value, slab_step, plane_step):
    pairs = []
    for slab in range(8 - slab_step):
        for plane in range(16 - plane_step):
            pairs.append((slab * 16 + plane, (slab + slab_step) * 16 + plane + plane_step))
    return lax.ppermute(value, AXES, pairs)


def swap(value, axis, second):
    count = lax.axis_size(axis)
    pairs = []
    for i in range(count):
        j = i + (1 if (i % 2 == 1) == second else -1)
        if 0 <= j < count:
            pairs.append((i, j))
    return lax.ppermute(value, axis, pairs)


def program(images, shifts, nodes):
    place = jnp.stack([lax.axis_index("slab"), lax.axis_index("plane")]).astype(jnp.int32)
    first, second, images, nodes = pack_rows(place, images, nodes)
    rows = swap(first, "plane", False), swap(second, "plane", True)
    first, second = pack_planes(place, images, nodes, *rows)
    planes = swap(first, "slab", False), swap(second, "slab", True)
    inner = inner_part(place, images, *rows)
    mismatch, own, to_slab, to_plane = local_part(place, *inner, *planes, *rows, nodes, shifts)

    def spaced(value, layout):
        rows = []
        for start, count, gap in layout:
            rows += [value[start : start + count], jnp.zeros((gap, 128), F32)]
        return jnp.concatenate(rows, 0)

    got = shifted(to_plane, 0, 1)
    to_slab = to_slab + spaced(got, ((24, 6, 18), (30, 6, 18), (39, 3, 5)))
    own = own + spaced(got, ((0, 6, 18), (6, 6, 18), (12, 6, 18), (18, 6, 18), (36, 3, 13)))
    got = shifted(to_slab, 1, 0)
    payload = own + spaced(got, ((0, 24, 24), (24, 24, 24), (48, 6, 10)))
    blocks = payload[None]
    for axis in range(3):
        blocks = jnp.concatenate([blocks, exchange(blocks, axis, False)], 0)
    parts = [blocks[:, start : start + count] for start, count in COLORS]
    for turn in range(2):
        parts = [
            jnp.concatenate([part, exchange(part, (color + turn) % 3, True)], 0)
            for color, part in enumerate(parts)
        ]
    last = []
    for color, part in enumerate(parts):
        last.append(exchange(part, (color + 2) % 3, True))
    other = []
    for part in parts:
        other.append(exchange(part, 3, False))
    data = arranged(early_kernel, place, parts + other)
    data = arranged(middle_kernel, place, last, data)
    other = []
    for part in last:
        other.append(exchange(part, 3, False))
    result = solve_part(place, nodes, data, other)
    return result, mismatch


def solution(mesh):
    in_specs = (
        P(None, "slab", "plane", None),
        P(None, "slab", "plane", None),
        P(None, "slab", "plane", None),
    )
    out_specs = (P(None, "slab", "plane", None), P("slab", "plane", None))
    return jax.shard_map(program, mesh=mesh, in_specs=in_specs, out_specs=out_specs, check_vma=False)
```
